32 devices in a mesh: parts: 2 (over x), blocks: 16 (over z, y, core).
Axes of the slice: x: 2, y: 2, z: 4, core: 2. Of those that a mesh axis runs over, the one named last changes fastest.
Arguments:
- coords: float32 [640, 3, 32768], P('blocks', None, 'parts'), parts along dimension 2
- pairs: int32 [2, 2048], replicated, may hold values from 0 to 639
- res_slot: int32 [640], replicated, may hold values from 0 to 639, each once
Outputs:
- distances: bfloat16 [4, 32768, 1024], P(None, ('parts', 'blocks')), parts along dimension 1
The draws below stay inside these ranges and needn't reach their ends.
There are 2 independent parts, one for each index of `parts`. The reference program is written for one: setup_inputs(seed, part) draws one part's arguments, and reference() takes and returns one part's arrays. A program takes and returns all parts, laid end to end along the dimension named above; an argument that names none is the same for every part. Nothing has to cross between parts.
All inputs are finite; a program needn't handle non-finite values.
Results may differ from the reference program's by a relative error of at most 0.0025.
Values may be sent and summed in bfloat16 or wider, within the bound.
No kernel may reach another device: no remote copies, remote signals or barrier semaphores. Data moves between devices by JAX's collectives and lax.ppermute only.
A program may use at most 192 MiB of HBM per device.

```python
import math
import jax
import jax.numpy as jnp
from jax import lax

RESIDUES = 640
CONTACTS = 2048
FB = 1024
ROUNDS = 4
FRAMES = 16384
N_BLOCKS = 16


def draw_coords(key, part):
    key_base, key_amp, key_noise = jax.random.split(jax.random.fold_in(key, 11), 3)
    base = 4.0 * jax.random.normal(key_base, (RESIDUES, 3, 1), jnp.float32)
    amplitude = jnp.exp(jax.random.uniform(key_amp, (1, 1, FRAMES), jnp.float32, math.log(0.4), math.log(5.0)))
    noise = jax.random.normal(key_noise, (RESIDUES, 3, FRAMES), jnp.float32)
    breath = jnp.ones((1, 1, FRAMES), jnp.float32)
    return base * breath + amplitude * noise


def with_ends(drawn, own_key, low, top_value):
    shape = drawn.shape
    place = [jax.random.randint(jax.random.fold_in(own_key, axis), (), 0, shape[axis]) for axis in range(len(shape))]
    drawn = drawn.at[tuple(place)].set(low)
    longest = shape.index(max(shape))
    place[longest] = (place[longest] + 1) % shape[longest]
    return drawn.at[tuple(place)].set(top_value)


def setup_inputs(seed: int = 0, part: int = 0) -> dict:
    arg_keys = jax.random.split(jax.random.key(seed), 4)
    part_keys = jax.random.split(jax.random.fold_in(arg_keys[3], part), 4)
    coords = draw_coords(jax.random.fold_in(jax.random.fold_in(arg_keys[3], part), 71), part)
    pairs = with_ends(jax.random.randint(arg_keys[1], (2, CONTACTS), 0, RESIDUES), jax.random.fold_in(arg_keys[1], 1), 0, RESIDUES - 1).astype(jnp.int32)
    res_slot = jax.random.permutation(arg_keys[2], RESIDUES).astype(jnp.int32)
    return dict(coords=coords, pairs=pairs, res_slot=res_slot)


def featurize(block, slot_first, slot_second):
    squared = jnp.zeros((slot_first.shape[0], block.shape[2]), jnp.float32)
    for component in range(3):
        offset = block[slot_first, component] - block[slot_second, component]
        squared = squared + offset * offset
    separation = jnp.sqrt(squared + 0.01)
    return jax.nn.sigmoid((8.0 - separation) / 1.5).T.astype(jnp.bfloat16)

def reference(coords, pairs, res_slot):
    position = jnp.zeros((RESIDUES,), jnp.int32).at[res_slot].set(jnp.arange(RESIDUES, dtype=jnp.int32))
    slot_first = position[pairs[0]]
    slot_second = position[pairs[1]]
    grouped = coords.reshape(RESIDUES, 3, N_BLOCKS, FB).transpose(2, 0, 1, 3)
    features = lax.map(lambda block: featurize(block, slot_first, slot_second), grouped)
    wide = features.astype(jnp.float32)
    norms = lax.optimization_barrier(jnp.sum(wide * wide, axis=-1))

    def tanimoto(items):
        own, visitor, own_norm, vis_norm = items
        intersection = jnp.dot(own, visitor.T, preferred_element_type=jnp.float32)
        ratio = intersection / (own_norm[:, None] + vis_norm[None, :] - intersection + 1e-06)
        return (1.0 - ratio).astype(jnp.bfloat16)
    results = []
    for offset_round in range(1, ROUNDS + 1):
        visitors = jnp.roll(features, offset_round, axis=0)
        vis_norms = jnp.roll(norms, offset_round, axis=0)
        block_dist = lax.map(tanimoto, (features, visitors, norms, vis_norms))
        results.append(block_dist.reshape(FRAMES, FB))
    return jnp.stack(results)
```

```python
import functools

import jax
import jax.numpy as jnp
from jax import lax
from jax.experimental import pallas as pl
from jax.experimental.pallas import tpu as pltpu
from jax.sharding import PartitionSpec as P

ROUNDS = 4
CHUNKS = 4
BF16_MAX = 3.3895313892515355e38


def permuted(shard, axis, to):
    count = lax.axis_size(axis)
    return lax.ppermute(shard, axis, [(i, to(i, count)) for i in range(count)])


def shift4(i, count):
    return (i + 4) % count


def swap1(i, count):
    return i ^ 1


def swap2(i, count):
    return i ^ 2


def features_kernel(x_ref, sel_ref, *refs, aliased):
    refs = refs[1:] if aliased else refs
    ft_ref, f_ref, norm_ref, split_ref = refs
    step = pl.program_id(0)
    groups, _, rows, width = x_ref.shape
    residues = groups * rows

    @pl.when(step == 0)
    def _():
        for component in range(3):
            rest = x_ref[:, component].reshape(residues, width)
            for term in range(3):
                part = jnp.clip(rest, -BF16_MAX, BF16_MAX).astype(jnp.bfloat16)
                split_ref[component, term * residues:(term + 1) * residues, :] = part
                rest = rest - part.astype(jnp.float32)
        norm_ref[...] = jnp.zeros_like(norm_ref)

    sel = sel_ref[...]
    sel = jnp.concatenate([sel, sel, sel], axis=1)
    squared = None
    for component in range(3):
        offset = jnp.dot(sel, split_ref[component], preferred_element_type=jnp.float32)
        squared = offset * offset if squared is None else squared + offset * offset
    separation = jnp.sqrt(squared + 0.01)
    feature = jax.nn.sigmoid((8.0 - separation) * (1.0 / 1.5)).astype(jnp.bfloat16)
    ft_ref[...] = feature
    own = feature.astype(jnp.float32).T
    f_ref[...] = own.astype(jnp.bfloat16)
    norm_ref[...] += jnp.sum(own * own, axis=1, keepdims=True)


def features_chunk(x, sel, own, chunk, chunks):
    groups, _, rows, width = x.shape
    contacts, residues = sel.shape
    tile = 256
    aliased = own is not None
    in_specs = [
        pl.BlockSpec(x.shape, lambda i: (0, 0, 0, 0)),
        pl.BlockSpec((tile, residues), lambda i: (i, 0)),
    ]
    args = [x, sel]
    if aliased:
        in_specs.append(pl.BlockSpec(memory_space=pl.ANY))
        args.append(own)
    return pl.pallas_call(
        functools.partial(features_kernel, aliased=aliased),
        grid=(contacts // tile,),
        in_specs=in_specs,
        out_specs=[
            pl.BlockSpec((tile, width), lambda i: (i, 0)),
            pl.BlockSpec((width, tile), lambda i: (chunk, i)),
            pl.BlockSpec((width, 1), lambda i: (0, 0)),
        ],
        out_shape=[
            jax.ShapeDtypeStruct((contacts, width), jnp.bfloat16),
            jax.ShapeDtypeStruct((width * chunks, contacts), jnp.bfloat16),
            jax.ShapeDtypeStruct((width, 1), jnp.float32),
        ],
        scratch_shapes=[pltpu.VMEM((3, 3 * residues, width), jnp.bfloat16)],
        input_output_aliases={2: 1} if aliased else {},
        name=f"features_{chunk}",
    )(*args)


def distance_kernel(bit_ref, own_ref, norm_ref, v4_ref, v2_ref, vx_ref, *refs, aliased):
    refs = refs[1:] if aliased else refs
    out_ref, vnorm_ref = refs
    bit = bit_ref[0]
    visitors = (
        lambda: vx_ref[bit],
        lambda: v2_ref[...],
        lambda: vx_ref[1 - bit],
        lambda: v4_ref[...],
    )

    @pl.when(pl.program_id(0) == 0)
    def _():
        for r, load in enumerate(visitors):
            wide = load().astype(jnp.float32)
            vnorm_ref[r, 0:1, :] = jnp.sum(wide * wide, axis=0, keepdims=True)

    own = own_ref[...]
    own_norm = norm_ref[...]
    for r, load in enumerate(visitors):
        inter = jnp.dot(own, load(), preferred_element_type=jnp.float32)
        ratio = inter / (own_norm + vnorm_ref[r, 0:1, :] - inter + 1e-06)
        out_ref[r] = (1.0 - ratio).astype(jnp.bfloat16)


def distance_chunk(bit, own, norms, v4, v2, vx, out, chunk, chunks):
    frames, contacts = own.shape
    width = v4.shape[1]
    tile = 256
    aliased = out is not None
    in_specs = [
        pl.BlockSpec(memory_space=pltpu.SMEM),
        pl.BlockSpec((tile, contacts), lambda i: (i, 0)),
        pl.BlockSpec((tile, 1), lambda i: (i, 0)),
        pl.BlockSpec((contacts, width), lambda i: (0, 0)),
        pl.BlockSpec((contacts, width), lambda i: (0, 0)),
        pl.BlockSpec((2, contacts, width), lambda i: (0, 0, 0)),
    ]
    args = [bit, own, norms, v4, v2, vx]
    if aliased:
        in_specs.append(pl.BlockSpec(memory_space=pl.ANY))
        args.append(out)
    return pl.pallas_call(
        functools.partial(distance_kernel, aliased=aliased),
        grid=(frames // tile,),
        in_specs=in_specs,
        out_specs=pl.BlockSpec((ROUNDS, tile, width), lambda i: (0, i, chunk)),
        out_shape=jax.ShapeDtypeStruct((ROUNDS, frames, width * chunks), jnp.bfloat16),
        scratch_shapes=[pltpu.VMEM((ROUNDS, 8, width), jnp.float32)],
        input_output_aliases={6: 0} if aliased else {},
        name=f"distances_{chunk}",
    )(*args)


def shards(coords, pairs, res_slot):
    count = lax.axis_size("blocks")
    index = lax.axis_index("blocks")
    res_local, _, frames = coords.shape
    per_block = frames // count
    width = per_block // CHUNKS
    residues = res_local * count

    split_coords = coords.reshape(res_local, 3, count, CHUNKS, width)
    arrived = []
    for j in range(CHUNKS):
        piece = split_coords[:, :, :, j].transpose(2, 1, 0, 3)
        got = lax.all_to_all(piece, "blocks", split_axis=0, concat_axis=0, tiled=True)
        if res_local % 8:
            got = got.transpose(1, 0, 2, 3).reshape(1, 3, residues, width)
        arrived.append(got)

    first = (pairs[0][:, None] == res_slot[None, :]).astype(jnp.float32)
    second = (pairs[1][:, None] == res_slot[None, :]).astype(jnp.float32)
    sel = (first - second).astype(jnp.bfloat16)

    low_core = (index & 1) == 0
    low_pair = (index & 2) == 0
    bit = (index & 1).astype(jnp.int32).reshape(1)

    own = None
    norms, visitors = [], []
    for j in range(CHUNKS):
        ft, own, norm = features_chunk(arrived[j], sel, own, j, CHUNKS)
        norms.append(norm)
        v4 = permuted(ft, "blocks", shift4)
        v2 = permuted(jnp.where(low_pair, ft, v4), "blocks", swap2)
        vx = permuted(jnp.stack([v2, jnp.where(low_core, ft, v4)]), "blocks", swap1)
        visitors.append((v4, v2, vx))
    norms = jnp.concatenate(norms, axis=0)
    out = None
    for j in range(CHUNKS):
        out = distance_chunk(bit, own, norms, *visitors[j], out, j, CHUNKS)
    return out


def solution(mesh):
    in_specs = (P("blocks", None, "parts"), P(), P())
    out_specs = P(None, ("parts", "blocks"), None)
    return jax.shard_map(shards, mesh=mesh, in_specs=in_specs, out_specs=out_specs, check_vma=False)
```

```python
import functools
import math

import jax
import jax.numpy as jnp
from jax import lax
from jax.experimental import pallas as pl
from jax.experimental.pallas import tpu as pltpu
from jax.sharding import PartitionSpec as P

ROUNDS = 4
VMEM_BYTES = 60000 * 1024


def permuted(shard, axis, to):
    count = lax.axis_size(axis)
    return lax.ppermute(shard, axis, [(i, to(i, count)) for i in range(count)])


def shift4(i, count):
    return (i + 4) % count


def swap1(i, count):
    return i ^ 1


def swap2(i, count):
    return i ^ 2


def largest_divisor(value, limit):
    return max(d for d in range(1, limit + 1) if value % d == 0)


def squares_kernel(slots_ref, x_ref, out_ref, atoms_ref, squares_ref, *, steps, tile, pitch):
    step = pl.program_id(0)
    per_step, _, rows, frames = x_ref.shape
    lanes = frames // 8

    @pl.when(step < steps)
    def _():
        def regroup(g, carry):
            for component in range(3):
                for top in range(0, rows, 8):
                    for s in range(8):
                        start = ((step * per_step + g) * rows + top) * 24 + component * 8 + s
                        atoms_ref[pl.ds(start, 8, stride=24), :] = x_ref[
                            g, component, top:top + 8, s * lanes:(s + 1) * lanes]
            return carry

        lax.fori_loop(0, per_step, regroup, 0)

    @pl.when(step >= steps)
    def _():
        base = (step - steps) * tile
        unroll = 16

        def contacts(i, carry):
            for u in range(unroll):
                c = i * unroll + u
                first = slots_ref[0, base + c]
                second = slots_ref[1, base + c]
                squared = None
                for row in (0, 8, 16):
                    offset = (atoms_ref[pl.ds(pl.multiple_of(first + row, 8), 8), :]
                              - atoms_ref[pl.ds(pl.multiple_of(second + row, 8), 8), :])
                    squared = offset * offset if squared is None else squared + offset * offset
                squares_ref[pl.ds(c, 8, stride=pitch), :] = squared
            return carry

        lax.fori_loop(0, tile // unroll, contacts, 0)
        for s in range(8):
            out_ref[s] = squares_ref[s * pitch:s * pitch + tile, :]


def squared_separations(x, slots24):
    groups, _, rows, frames = x.shape
    contacts = slots24.shape[1]
    per_step = largest_divisor(groups, max(1, 160 // rows))
    steps = groups // per_step
    tile = 512
    pitch = tile + 8
    return pl.pallas_call(
        functools.partial(squares_kernel, steps=steps, tile=tile, pitch=pitch),
        grid_spec=pltpu.PrefetchScalarGridSpec(
            num_scalar_prefetch=1,
            grid=(steps + contacts // tile,),
            in_specs=[pl.BlockSpec((per_step, 3, rows, frames),
                                   lambda i, s: (jnp.minimum(i, steps - 1), 0, 0, 0))],
            out_specs=pl.BlockSpec((8, tile, frames // 8),
                                   lambda i, s: (0, jnp.maximum(i - steps, 0), 0)),
            scratch_shapes=[
                pltpu.VMEM((groups * rows * 24, frames // 8), jnp.float32),
                pltpu.VMEM((8 * pitch, frames // 8), jnp.float32),
            ],
        ),
        out_shape=jax.ShapeDtypeStruct((8, contacts, frames // 8), jnp.float32),
        compiler_params=pltpu.CompilerParams(vmem_limit_bytes=VMEM_BYTES),
        name="squares",
    )(slots24, x)


def features_kernel(squared_ref, *refs, aliased):
    refs = refs[1:] if aliased else refs
    ft_ref, f_ref, norm_ref = refs
    lanes = squared_ref.shape[2]

    @pl.when(pl.program_id(0) == 0)
    def _():
        norm_ref[...] = jnp.zeros_like(norm_ref)

    for s in range(squared_ref.shape[0]):
        span = slice(s * lanes, (s + 1) * lanes)
        squared = jnp.minimum(squared_ref[s] + 0.01, 1e30)
        separation = squared * lax.rsqrt(squared)
        scale = math.log2(math.e) / 1.5
        feature = 1.0 / (1.0 + jnp.exp2(separation * scale - 8.0 * scale))
        feature = feature.astype(jnp.bfloat16)
        ft_ref[:, span] = feature
        own = feature.astype(jnp.float32).T
        f_ref[span, :] = own.astype(jnp.bfloat16)
        norm_ref[span, :] += jnp.sum(own * own, axis=1, keepdims=True)


def features_chunk(squared, own, start, width):
    _, contacts, lanes = squared.shape
    tile = 1024
    part = width // lanes
    block = start // width
    aliased = own is not None
    in_specs = [pl.BlockSpec((part, tile, lanes), lambda i: (block, i, 0))]
    args = [squared]
    if aliased:
        in_specs.append(pl.BlockSpec(memory_space=pl.ANY))
        args.append(own)
    return pl.pallas_call(
        functools.partial(features_kernel, aliased=aliased),
        grid=(contacts // tile,),
        in_specs=in_specs,
        out_specs=[
            pl.BlockSpec((tile, width), lambda i: (i, 0)),
            pl.BlockSpec((width, tile), lambda i: (block, i)),
            pl.BlockSpec((width, 1), lambda i: (0, 0)),
        ],
        out_shape=[
            jax.ShapeDtypeStruct((contacts, width), jnp.bfloat16),
            jax.ShapeDtypeStruct((8 * lanes, contacts), jnp.bfloat16),
            jax.ShapeDtypeStruct((width, 1), jnp.float32),
        ],
        input_output_aliases={1: 1} if aliased else {},
        compiler_params=pltpu.CompilerParams(vmem_limit_bytes=VMEM_BYTES),
        name=f"features_{start}",
    )(*args)


def distance_kernel(bit_ref, own_ref, norm_ref, v4_ref, v2_ref, vx_ref, *refs, aliased):
    refs = refs[1:] if aliased else refs
    out_ref, vnorm_ref = refs
    bit = bit_ref[0]
    visitors = (
        lambda: vx_ref[bit],
        lambda: v2_ref[...],
        lambda: vx_ref[1 - bit],
        lambda: v4_ref[...],
    )

    @pl.when(pl.program_id(0) == 0)
    def _():
        for r, load in enumerate(visitors):
            wide = load().astype(jnp.float32)
            vnorm_ref[r, 0:1, :] = jnp.sum(wide * wide, axis=0, keepdims=True)

    own = own_ref[...]
    own_norm = norm_ref[...]
    for r, load in enumerate(visitors):
        inter = jnp.dot(own, load(), preferred_element_type=jnp.float32)
        ratio = inter / (own_norm + vnorm_ref[r, 0:1, :] - inter + 1e-06)
        out_ref[r] = (1.0 - ratio).astype(jnp.bfloat16)


def distance_chunk(bit, own, norms, v4, v2, vx, out, start):
    frames, contacts = own.shape
    width = v4.shape[1]
    tile = 256
    block = start // width
    aliased = out is not None
    in_specs = [
        pl.BlockSpec(memory_space=pltpu.SMEM),
        pl.BlockSpec((tile, contacts), lambda i: (i, 0)),
        pl.BlockSpec((tile, 1), lambda i: (i, 0)),
        pl.BlockSpec((contacts, width), lambda i: (0, 0)),
        pl.BlockSpec((contacts, width), lambda i: (0, 0)),
        pl.BlockSpec((2, contacts, width), lambda i: (0, 0, 0)),
    ]
    args = [bit, own, norms, v4, v2, vx]
    if aliased:
        in_specs.append(pl.BlockSpec(memory_space=pl.ANY))
        args.append(out)
    return pl.pallas_call(
        functools.partial(distance_kernel, aliased=aliased),
        grid=(frames // tile,),
        in_specs=in_specs,
        out_specs=pl.BlockSpec((ROUNDS, tile, width), lambda i: (0, i, block)),
        out_shape=jax.ShapeDtypeStruct((ROUNDS, frames, frames), jnp.bfloat16),
        scratch_shapes=[pltpu.VMEM((ROUNDS, 8, width), jnp.float32)],
        input_output_aliases={6: 0} if aliased else {},
        compiler_params=pltpu.CompilerParams(vmem_limit_bytes=VMEM_BYTES),
        name=f"distances_{start}",
    )(*args)


def contact_slots(pairs, res_slot):
    hits = pairs[:, :, None] == res_slot[None, None, :]
    places = jnp.arange(res_slot.shape[0], dtype=jnp.int32)
    return jnp.sum(jnp.where(hits, places, 0), axis=2, dtype=jnp.int32)


def shards(coords, pairs, res_slot):
    count = lax.axis_size("blocks")
    index = lax.axis_index("blocks")
    res_local, _, frames = coords.shape
    per_block = frames // count
    lanes = per_block // 8
    residues = res_local * count
    widths = [lanes * n for n in (2, 2, 2, 1, 1)]

    pieces = coords.reshape(res_local, 3, count, per_block).transpose(2, 1, 0, 3)
    arrived = lax.all_to_all(pieces, "blocks", split_axis=0, concat_axis=0, tiled=True)
    if res_local % 8:
        arrived = arrived.transpose(0, 2, 1, 3).reshape(residues // 8, 8, 3, per_block)
        arrived = arrived.transpose(0, 2, 1, 3)
    slots24 = contact_slots(pairs, res_slot) * 24
    squared = squared_separations(arrived, slots24)

    low_core = (index & 1) == 0
    low_pair = (index & 2) == 0
    bit = (index & 1).astype(jnp.int32).reshape(1)

    own = None
    norms, visitors = [], []
    start = 0
    for width in widths:
        ft, own, norm = features_chunk(squared, own, start, width)
        norms.append(norm)
        v4 = permuted(ft, "blocks", shift4)
        v2 = permuted(jnp.where(low_pair, ft, v4), "blocks", swap2)
        vx = permuted(jnp.stack([v2, jnp.where(low_core, ft, v4)]), "blocks", swap1)
        visitors.append((start, v4, v2, vx))
        start += width
    norms = jnp.concatenate(norms, axis=0)
    out = None
    for start, v4, v2, vx in visitors:
        out = distance_chunk(bit, own, norms, v4, v2, vx, out, start)
    return out


def solution(mesh):
    in_specs = (P("blocks", None, "parts"), P(), P())
    out_specs = P(None, ("parts", "blocks"), None)
    return jax.shard_map(shards, mesh=mesh, in_specs=in_specs, out_specs=out_specs, check_vma=False)
```

```python
import functools
import math

import jax
import jax.numpy as jnp
from jax import lax
from jax.experimental import pallas as pl
from jax.experimental.pallas import tpu as pltpu
from jax.sharding import PartitionSpec as P


ROUNDS = 4
VMEM_BYTES = 58 * 1024 * 1024


def permuted(shard, axis, to):
    count = lax.axis_size(axis)
    return lax.ppermute(shard, axis, [(i, to(i, count)) for i in range(count)])


def shift4(i, count):
    return (i + 4) % count


def swap1(i, count):
    return i ^ 1


def swap2(i, count):
    return i ^ 2


def largest_divisor(value, limit):
    return max(d for d in range(1, limit + 1) if value % d == 0)


def features_kernel(slots_ref, x_ref, *refs, steps, tile, pitch):
    *ft_refs, atoms_ref, squares_ref = refs
    step = pl.program_id(0)
    per_step, _, rows, frames = x_ref.shape
    lanes = frames // 8

    @pl.when(step < steps)
    def _():
        def regroup(g, carry):
            for component in range(3):
                for top in range(0, rows, 8):
                    for s in range(8):
                        start = ((step * per_step + g) * rows + top) * 24 + component * 8 + s
                        atoms_ref[pl.ds(start, 8, stride=24), :] = x_ref[
                            g, component, top:top + 8, s * lanes:(s + 1) * lanes]
            return carry

        lax.fori_loop(0, per_step, regroup, 0)

    @pl.when(step >= steps)
    def _():
        base = (step - steps) * tile
        unroll = 16

        def contacts(i, carry):
            for u in range(unroll):
                c = i * unroll + u
                first = slots_ref[0, base + c]
                second = slots_ref[1, base + c]
                squared = None
                for row in (0, 8, 16):
                    offset = (atoms_ref[pl.ds(pl.multiple_of(first + row, 8), 8), :]
                              - atoms_ref[pl.ds(pl.multiple_of(second + row, 8), 8), :])
                    squared = offset * offset if squared is None else squared + offset * offset
                squares_ref[pl.ds(c, 8, stride=pitch), :] = squared
            return carry

        lax.fori_loop(0, tile // unroll, contacts, 0)
        s = 0
        for ft_ref in ft_refs:
            for left in range(0, ft_ref.shape[1], lanes):
                squared = jnp.minimum(squares_ref[s * pitch:s * pitch + tile, :] + 0.01, 1e30)
                separation = squared * lax.rsqrt(squared)
                scale = math.log2(math.e) / 1.5
                feature = 1.0 / (1.0 + jnp.exp2(separation * scale - 8.0 * scale))
                ft_ref[:, left:left + lanes] = feature.astype(jnp.bfloat16)
                s += 1


def features_of(x, slots24, widths):
    groups, _, rows, frames = x.shape
    contacts = slots24.shape[1]
    per_step = largest_divisor(groups, max(1, 160 // rows))
    steps = groups // per_step
    tile = 512
    pitch = tile + 8
    return pl.pallas_call(
        functools.partial(features_kernel, steps=steps, tile=tile, pitch=pitch),
        grid_spec=pltpu.PrefetchScalarGridSpec(
            num_scalar_prefetch=1,
            grid=(steps + contacts // tile,),
            in_specs=[pl.BlockSpec((per_step, 3, rows, frames),
                                   lambda i, s: (jnp.minimum(i, steps - 1), 0, 0, 0))],
            out_specs=[pl.BlockSpec((tile, width), lambda i, s: (jnp.maximum(i - steps, 0), 0))
                       for width in widths],
            scratch_shapes=[
                pltpu.VMEM((groups * rows * 24, frames // 8), jnp.float32),
                pltpu.VMEM((8 * pitch, frames // 8), jnp.float32),
            ],
        ),
        out_shape=[jax.ShapeDtypeStruct((contacts, width), jnp.bfloat16) for width in widths],
        compiler_params=pltpu.CompilerParams(vmem_limit_bytes=VMEM_BYTES),
        name="features",
    )(slots24, x)


def own_kernel(*refs):
    *ft_refs, f_ref, norm_ref = refs

    @pl.when(pl.program_id(0) == 0)
    def _():
        norm_ref[...] = jnp.zeros_like(norm_ref)

    row = 0
    for ft_ref in ft_refs:
        width = ft_ref.shape[1]
        own = ft_ref[...].astype(jnp.float32).T
        f_ref[row:row + width, :] = own.astype(jnp.bfloat16)
        norm_ref[row:row + width, :] += jnp.sum(own * own, axis=1, keepdims=True)
        row += width


def own_features(fts):
    contacts = fts[0].shape[0]
    frames = sum(ft.shape[1] for ft in fts)
    tile = 512
    return pl.pallas_call(
        own_kernel,
        grid=(contacts // tile,),
        in_specs=[pl.BlockSpec((tile, ft.shape[1]), lambda i: (i, 0)) for ft in fts],
        out_specs=[
            pl.BlockSpec((frames, tile), lambda i: (0, i)),
            pl.BlockSpec((frames, 1), lambda i: (0, 0)),
        ],
        out_shape=[
            jax.ShapeDtypeStruct((frames, contacts), jnp.bfloat16),
            jax.ShapeDtypeStruct((frames, 1), jnp.float32),
        ],
        compiler_params=pltpu.CompilerParams(vmem_limit_bytes=VMEM_BYTES),
        name="own_features",
    )(*fts)


def pick_kernel(flag_ref, first_ref, second_ref, *refs):
    out_ref, sem = refs[-2:]

    @pl.when(flag_ref[0] == 1)
    def _():
        pltpu.make_async_copy(first_ref, out_ref, sem).start()

    @pl.when(flag_ref[0] != 1)
    def _():
        pltpu.make_async_copy(second_ref, out_ref, sem).start()

    pltpu.make_async_copy(first_ref, out_ref, sem).wait()


def pick(flag, first, second, after):
    anywhere = pl.BlockSpec(memory_space=pl.ANY)
    return pl.pallas_call(
        pick_kernel,
        in_specs=[pl.BlockSpec(memory_space=pltpu.SMEM)] + [anywhere] * (2 + len(after)),
        out_specs=anywhere,
        out_shape=jax.ShapeDtypeStruct(first.shape, first.dtype),
        scratch_shapes=[pltpu.SemaphoreType.DMA(())],
        name="pick",
    )(flag, first, second, *after)


def pack_kernel(flag_ref, v2_ref, first_ref, second_ref, *refs):
    out_ref, sems = refs[-2:]
    pltpu.make_async_copy(v2_ref, out_ref.at[0], sems.at[0]).start()

    @pl.when(flag_ref[0] == 1)
    def _():
        pltpu.make_async_copy(first_ref, out_ref.at[1], sems.at[1]).start()

    @pl.when(flag_ref[0] != 1)
    def _():
        pltpu.make_async_copy(second_ref, out_ref.at[1], sems.at[1]).start()

    pltpu.make_async_copy(v2_ref, out_ref.at[0], sems.at[0]).wait()
    pltpu.make_async_copy(first_ref, out_ref.at[1], sems.at[1]).wait()


def pack(flag, v2, first, second, after):
    anywhere = pl.BlockSpec(memory_space=pl.ANY)
    return pl.pallas_call(
        pack_kernel,
        in_specs=[pl.BlockSpec(memory_space=pltpu.SMEM)] + [anywhere] * (3 + len(after)),
        out_specs=anywhere,
        out_shape=jax.ShapeDtypeStruct((2,) + first.shape, first.dtype),
        scratch_shapes=[pltpu.SemaphoreType.DMA((2,))],
        name="pack",
    )(flag, v2, first, second, *after)


def distance_kernel(bit_ref, own_ref, norm_ref, v4_ref, v2_ref, vx_ref, *refs, aliased):
    refs = refs[1:] if aliased else refs
    out_ref, token_ref, vnorm_ref = refs
    bit = bit_ref[0]
    visitors = (
        lambda: vx_ref[bit],
        lambda: v2_ref[...],
        lambda: vx_ref[1 - bit],
        lambda: v4_ref[...],
    )

    @pl.when(pl.program_id(0) == 0)
    def _():
        for r, load in enumerate(visitors):
            wide = load().astype(jnp.float32)
            vnorm_ref[r, 0:1, :] = jnp.sum(wide * wide, axis=0, keepdims=True)
        token_ref[...] = jnp.zeros_like(token_ref)

    own = own_ref[...]
    own_norm = norm_ref[...]
    for r, load in enumerate(visitors):
        inter = jnp.dot(own, load(), preferred_element_type=jnp.float32)
        ratio = inter / (own_norm + vnorm_ref[r, 0:1, :] - inter + 1e-06)
        out_ref[r] = (1.0 - ratio).astype(jnp.bfloat16)


def distance_chunk(bit, own, norms, v4, v2, vx, out, start):
    frames, contacts = own.shape
    width = v4.shape[1]
    tile = 256
    block = start // width
    aliased = out is not None
    in_specs = [
        pl.BlockSpec(memory_space=pltpu.SMEM),
        pl.BlockSpec((tile, contacts), lambda i: (i, 0)),
        pl.BlockSpec((tile, 1), lambda i: (i, 0)),
        pl.BlockSpec((contacts, width), lambda i: (0, 0)),
        pl.BlockSpec((contacts, width), lambda i: (0, 0)),
        pl.BlockSpec((2, contacts, width), lambda i: (0, 0, 0)),
    ]
    args = [bit, own, norms, v4, v2, vx]
    if aliased:
        in_specs.append(pl.BlockSpec(memory_space=pl.ANY))
        args.append(out)
    return pl.pallas_call(
        functools.partial(distance_kernel, aliased=aliased),
        grid=(frames // tile,),
        in_specs=in_specs,
        out_specs=[
            pl.BlockSpec((ROUNDS, tile, width), lambda i: (0, i, block)),
            pl.BlockSpec((8, 128), lambda i: (0, 0)),
        ],
        out_shape=[
            jax.ShapeDtypeStruct((ROUNDS, frames, frames), jnp.bfloat16),
            jax.ShapeDtypeStruct((8, 128), jnp.float32),
        ],
        scratch_shapes=[pltpu.VMEM((ROUNDS, 8, width), jnp.float32)],
        input_output_aliases={6: 0} if aliased else {},
        compiler_params=pltpu.CompilerParams(vmem_limit_bytes=VMEM_BYTES),
    )(*args)


def contact_slots(pairs, res_slot):
    hits = pairs[:, :, None] == res_slot[None, None, :]
    places = jnp.arange(res_slot.shape[0], dtype=jnp.int32)
    return jnp.sum(jnp.where(hits, places, 0), axis=2, dtype=jnp.int32)


def exchanged(pieces):
    return lax.all_to_all(pieces, "blocks", split_axis=0, concat_axis=0, tiled=True)


def gathered_coords(coords, count):
    res_local, _, frames = coords.shape
    per_block = frames // count
    blocks = coords.reshape(res_local, 3, count, per_block)
    extent = jnp.max(jnp.abs(coords))
    scaled = 1.0 / per_block
    spread = jnp.sum(blocks * blocks, axis=3) * scaled - (jnp.sum(blocks, axis=3) * scaled) ** 2
    spread = jnp.min(jnp.mean(spread, axis=(0, 1)))
    fine = (extent <= 64.0) & (spread >= 6e-5 * extent * extent)
    pieces = blocks.transpose(2, 1, 0, 3)
    narrow = jnp.where(fine, pieces, jnp.inf).astype(jnp.float16)
    narrow = exchanged(narrow)
    all_fine = jnp.all(narrow[:, 0, 0, 0].astype(jnp.float32) < jnp.inf)
    return lax.cond(all_fine, lambda: narrow.astype(jnp.float32), lambda: exchanged(pieces))


def shards(coords, pairs, res_slot):
    count = lax.axis_size("blocks")
    index = lax.axis_index("blocks")
    res_local, _, frames = coords.shape
    per_block = frames // count
    lanes = per_block // 8
    residues = res_local * count
    widths = [lanes * n for n in (2, 2, 2, 1, 1)]

    arrived = gathered_coords(coords, count)
    if res_local % 8:
        arrived = arrived.transpose(0, 2, 1, 3).reshape(residues // 8, 8, 3, per_block)
        arrived = arrived.transpose(0, 2, 1, 3)
    slots24 = contact_slots(pairs, res_slot) * 24
    fts = features_of(arrived, slots24, widths)
    bit = (index & 1).astype(jnp.int32).reshape(1)
    low_core = 1 - bit
    low_pair = 1 - ((index >> 1) & 1).astype(jnp.int32).reshape(1)

    v4s = []
    for ft in fts:
        v4s.append(permuted(ft, "blocks", shift4))
    own, norms = own_features(fts)
    out = None
    tokens = []
    start = 0
    for j, (ft, v4) in enumerate(zip(fts, v4s)):
        after = tokens[j - 2:j - 1] if j >= 2 else [norms]
        v2 = permuted(pick(low_pair, ft, v4, after), "blocks", swap2)
        vx = permuted(pack(low_core, v2, ft, v4, []), "blocks", swap1)
        out, token = distance_chunk(bit, own, norms, v4, v2, vx, out, start)
        tokens.append(token)
        start += ft.shape[1]
    return out


def solution(mesh):
    in_specs = (P("blocks", None, "parts"), P(), P())
    out_specs = P(None, ("parts", "blocks"), None)
    return jax.shard_map(shards, mesh=mesh, in_specs=in_specs, out_specs=out_specs, check_vma=False)
```

```python
import functools
import math

import jax
import jax.numpy as jnp
from jax import lax
from jax.experimental import pallas as pl
from jax.experimental.pallas import tpu as pltpu
from jax.sharding import PartitionSpec as P


ROUNDS = 4
VMEM_BYTES = 58 * 1024 * 1024


def permuted(shard, axis, to):
    count = lax.axis_size(axis)
    return lax.ppermute(shard, axis, [(i, to(i, count)) for i in range(count)])


def shift4(i, count):
    return (i + 4) % count


def swap1(i, count):
    return i ^ 1


def swap2(i, count):
    return i ^ 2


def largest_divisor(value, limit):
    return max(d for d in range(1, limit + 1) if value % d == 0)


def features_kernel(slots_ref, x_ref, *refs, steps, tile, pitch):
    *ft_refs, atoms_ref, squares_ref = refs
    step = pl.program_id(0)
    per_step, _, rows, frames = x_ref.shape
    lanes = frames // 8

    @pl.when(step < steps)
    def _():
        def regroup(g, carry):
            for component in range(3):
                for top in range(0, rows, 8):
                    for s in range(8):
                        start = ((step * per_step + g) * rows + top) * 24 + component * 8 + s
                        atoms_ref[pl.ds(start, 8, stride=24), :] = x_ref[
                            g, component, top:top + 8, s * lanes:(s + 1) * lanes]
            return carry

        lax.fori_loop(0, per_step, regroup, 0)

    @pl.when(step >= steps)
    def _():
        base = (step - steps) * tile
        unroll = 16

        def contacts(i, carry):
            for u in range(unroll):
                c = i * unroll + u
                first = slots_ref[0, base + c]
                second = slots_ref[1, base + c]
                squared = None
                for row in (0, 8, 16):
                    offset = (atoms_ref[pl.ds(pl.multiple_of(first + row, 8), 8), :]
                              - atoms_ref[pl.ds(pl.multiple_of(second + row, 8), 8), :])
                    squared = offset * offset if squared is None else squared + offset * offset
                squares_ref[pl.ds(c, 8, stride=pitch), :] = squared
            return carry

        lax.fori_loop(0, tile // unroll, contacts, 0)
        s = 0
        for ft_ref in ft_refs:
            for left in range(0, ft_ref.shape[1], lanes):
                squared = jnp.minimum(squares_ref[s * pitch:s * pitch + tile, :] + 0.01, 1e30)
                separation = squared * lax.rsqrt(squared)
                scale = math.log2(math.e) / 1.5
                feature = 1.0 / (1.0 + jnp.exp2(separation * scale - 8.0 * scale))
                ft_ref[:, left:left + lanes] = feature.astype(jnp.bfloat16)
                s += 1


def features_of(x, slots24, widths):
    groups, _, rows, frames = x.shape
    contacts = slots24.shape[1]
    per_step = largest_divisor(groups, max(1, 160 // rows))
    steps = groups // per_step
    tile = 512
    pitch = tile + 8
    return pl.pallas_call(
        functools.partial(features_kernel, steps=steps, tile=tile, pitch=pitch),
        grid_spec=pltpu.PrefetchScalarGridSpec(
            num_scalar_prefetch=1,
            grid=(steps + contacts // tile,),
            in_specs=[pl.BlockSpec((per_step, 3, rows, frames),
                                   lambda i, s: (jnp.minimum(i, steps - 1), 0, 0, 0))],
            out_specs=[pl.BlockSpec((tile, width), lambda i, s: (jnp.maximum(i - steps, 0), 0))
                       for width in widths],
            scratch_shapes=[
                pltpu.VMEM((groups * rows * 24, frames // 8), jnp.float32),
                pltpu.VMEM((8 * pitch, frames // 8), jnp.float32),
            ],
        ),
        out_shape=[jax.ShapeDtypeStruct((contacts, width), jnp.bfloat16) for width in widths],
        compiler_params=pltpu.CompilerParams(vmem_limit_bytes=VMEM_BYTES),
        name="features",
    )(slots24, x)


def own_kernel(*refs):
    *ft_refs, f_ref, norm_ref = refs

    @pl.when(pl.program_id(0) == 0)
    def _():
        norm_ref[...] = jnp.zeros_like(norm_ref)

    row = 0
    for ft_ref in ft_refs:
        width = ft_ref.shape[1]
        own = ft_ref[...].astype(jnp.float32).T
        f_ref[row:row + width, :] = own.astype(jnp.bfloat16)
        norm_ref[row:row + width, :] += jnp.sum(own * own, axis=1, keepdims=True)
        row += width


def own_features(fts):
    contacts = fts[0].shape[0]
    frames = sum(ft.shape[1] for ft in fts)
    tile = 512
    return pl.pallas_call(
        own_kernel,
        grid=(contacts // tile,),
        in_specs=[pl.BlockSpec((tile, ft.shape[1]), lambda i: (i, 0)) for ft in fts],
        out_specs=[
            pl.BlockSpec((frames, tile), lambda i: (0, i)),
            pl.BlockSpec((frames, 1), lambda i: (0, 0)),
        ],
        out_shape=[
            jax.ShapeDtypeStruct((frames, contacts), jnp.bfloat16),
            jax.ShapeDtypeStruct((frames, 1), jnp.float32),
        ],
        compiler_params=pltpu.CompilerParams(vmem_limit_bytes=VMEM_BYTES),
        name="own_features",
    )(*fts)


def pick_kernel(flag_ref, first_ref, second_ref, *refs):
    out_ref, rows_ref, in_sems, out_sems = refs[-4:]
    parts = in_sems.shape[0]
    size = rows_ref.shape[0] // parts
    spans = [pl.ds(k * size, size) for k in range(parts)]

    def fetch(source_ref):
        for k, span in enumerate(spans):
            pltpu.make_async_copy(source_ref.at[span], rows_ref.at[span], in_sems.at[k]).start()

    @pl.when(flag_ref[0] == 1)
    def _():
        fetch(first_ref)

    @pl.when(flag_ref[0] != 1)
    def _():
        fetch(second_ref)

    for k, span in enumerate(spans):
        pltpu.make_async_copy(first_ref.at[span], rows_ref.at[span], in_sems.at[k]).wait()
        pltpu.make_async_copy(rows_ref.at[span], out_ref.at[span], out_sems.at[k]).start()
    for k, span in enumerate(spans):
        pltpu.make_async_copy(rows_ref.at[span], out_ref.at[span], out_sems.at[k]).wait()


def pick(flag, first, second, after):
    anywhere = pl.BlockSpec(memory_space=pl.ANY)
    return pl.pallas_call(
        pick_kernel,
        in_specs=[pl.BlockSpec(memory_space=pltpu.SMEM)] + [anywhere] * (2 + len(after)),
        out_specs=anywhere,
        out_shape=jax.ShapeDtypeStruct(first.shape, first.dtype),
        scratch_shapes=[pltpu.VMEM(first.shape, first.dtype), pltpu.SemaphoreType.DMA((4,)),
                        pltpu.SemaphoreType.DMA((4,))],
        name="pick",
    )(flag, first, second, *after)


def distance_kernel(bit_ref, own_ref, norm_ref, v4_ref, v2_ref, vx_ref, vy_ref, *refs, aliased):
    refs = refs[1:] if aliased else refs
    out_ref, token_ref, vnorm_ref = refs
    high_core = bit_ref[0] == 1
    visitors = (
        lambda: jnp.where(high_core, vy_ref[...], vx_ref[...]),
        lambda: v2_ref[...],
        lambda: jnp.where(high_core, vx_ref[...], vy_ref[...]),
        lambda: v4_ref[...],
    )

    @pl.when(pl.program_id(0) == 0)
    def _():
        for r, load in enumerate(visitors):
            wide = load().astype(jnp.float32)
            vnorm_ref[r, 0:1, :] = jnp.sum(wide * wide, axis=0, keepdims=True)
        token_ref[...] = jnp.zeros_like(token_ref)

    own = own_ref[...]
    own_norm = norm_ref[...]
    for r, load in enumerate(visitors):
        inter = jnp.dot(own, load(), preferred_element_type=jnp.float32)
        ratio = inter / (own_norm + vnorm_ref[r, 0:1, :] - inter + 1e-06)
        out_ref[r] = (1.0 - ratio).astype(jnp.bfloat16)


def distance_chunk(bit, own, norms, v4, v2, vx, vy, out, start):
    frames, contacts = own.shape
    width = v4.shape[1]
    tile = 256
    block = start // width
    aliased = out is not None
    in_specs = [
        pl.BlockSpec(memory_space=pltpu.SMEM),
        pl.BlockSpec((tile, contacts), lambda i: (i, 0)),
        pl.BlockSpec((tile, 1), lambda i: (i, 0)),
    ] + [pl.BlockSpec((contacts, width), lambda i: (0, 0))] * 4
    args = [bit, own, norms, v4, v2, vx, vy]
    if aliased:
        in_specs.append(pl.BlockSpec(memory_space=pl.ANY))
        args.append(out)
    return pl.pallas_call(
        functools.partial(distance_kernel, aliased=aliased),
        grid=(frames // tile,),
        in_specs=in_specs,
        out_specs=[
            pl.BlockSpec((ROUNDS, tile, width), lambda i: (0, i, block)),
            pl.BlockSpec((8, 128), lambda i: (0, 0)),
        ],
        out_shape=[
            jax.ShapeDtypeStruct((ROUNDS, frames, frames), jnp.bfloat16),
            jax.ShapeDtypeStruct((8, 128), jnp.float32),
        ],
        scratch_shapes=[pltpu.VMEM((ROUNDS, 8, width), jnp.float32)],
        input_output_aliases={7: 0} if aliased else {},
        compiler_params=pltpu.CompilerParams(vmem_limit_bytes=VMEM_BYTES),
    )(*args)


def contact_slots(pairs, res_slot):
    hits = pairs[:, :, None] == res_slot[None, None, :]
    places = jnp.arange(res_slot.shape[0], dtype=jnp.int32)
    return jnp.sum(jnp.where(hits, places, 0), axis=2, dtype=jnp.int32)


def split_kernel(x_ref, pieces_ref, fine_ref, extent_ref, spread_ref):
    step = pl.program_id(0)
    count, _, _, frames = pieces_ref.shape

    @pl.when(step == 0)
    def _():
        extent_ref[...] = jnp.zeros_like(extent_ref)
        spread_ref[...] = jnp.full_like(spread_ref, jnp.inf)

    for k in range(count):
        x = x_ref[:, :, k * frames:(k + 1) * frames]
        pieces_ref[k] = x
        extent_ref[...] = jnp.maximum(extent_ref[...], jnp.max(jnp.abs(x), axis=(0, 2), keepdims=True)[0])
        mean = jnp.sum(x, axis=2, keepdims=True) * (1.0 / frames)
        square = jnp.sum(x * x, axis=2, keepdims=True) * (1.0 / frames)
        spread = jnp.mean(square - mean * mean, axis=(0, 1), keepdims=True)[0]
        spread_ref[...] = jnp.minimum(spread_ref[...], spread)

    @pl.when(step == pl.num_programs(0) - 1)
    def _():
        extent = jnp.max(extent_ref[...], axis=0, keepdims=True)
        fine = (extent <= 64.0) & (spread_ref[...] >= 6e-5 * extent * extent)
        fine_ref[...] = jnp.where(fine, 1.0, 0.0)


def split_blocks(coords, count):
    _, rows, frames = coords.shape
    per_block = frames // count
    per_step = 2 if count % 2 == 0 else 1
    return pl.pallas_call(
        split_kernel,
        grid=(count // per_step,),
        in_specs=[pl.BlockSpec((3, rows, per_step * per_block), lambda i: (0, 0, i))],
        out_specs=[
            pl.BlockSpec((per_step, 3, rows, per_block), lambda i: (i, 0, 0, 0)),
            pl.BlockSpec((1, 1), lambda i: (0, 0)),
        ],
        out_shape=[
            jax.ShapeDtypeStruct((count, 3, rows, per_block), jnp.float32),
            jax.ShapeDtypeStruct((1, 1), jnp.float32),
        ],
        scratch_shapes=[pltpu.VMEM((rows, 1), jnp.float32), pltpu.VMEM((1, 1), jnp.float32)],
        compiler_params=pltpu.CompilerParams(vmem_limit_bytes=VMEM_BYTES),
        name="split_blocks",
    )(coords)


def exchanged(pieces):
    return lax.all_to_all(pieces, "blocks", split_axis=0, concat_axis=0, tiled=True)


def gathered_coords(coords, count):
    pieces, fine = split_blocks(coords.transpose(1, 0, 2), count)
    narrow = exchanged(jnp.where(fine[0, 0] > 0.5, pieces, jnp.inf).astype(jnp.float16))
    all_fine = jnp.all(narrow[:, 0, 0, 0].astype(jnp.float32) < jnp.inf)
    return lax.cond(all_fine, lambda: narrow.astype(jnp.float32), lambda: exchanged(pieces))


def shards(coords, pairs, res_slot):
    count = lax.axis_size("blocks")
    index = lax.axis_index("blocks")
    res_local, _, frames = coords.shape
    per_block = frames // count
    lanes = per_block // 8
    residues = res_local * count
    widths = [lanes * n for n in (2, 2, 2, 1, 1)]

    arrived = gathered_coords(coords, count)
    if res_local % 8:
        arrived = arrived.transpose(0, 2, 1, 3).reshape(residues // 8, 8, 3, per_block)
        arrived = arrived.transpose(0, 2, 1, 3)
    slots24 = contact_slots(pairs, res_slot) * 24
    fts = features_of(arrived, slots24, widths)
    bit = (index & 1).astype(jnp.int32).reshape(1)
    low_core = 1 - bit
    low_pair = 1 - ((index >> 1) & 1).astype(jnp.int32).reshape(1)

    v4s = []
    for ft in fts:
        v4s.append(permuted(ft, "blocks", shift4))
    own, norms = own_features(fts)
    out = None
    tokens = []
    start = 0
    for j, (ft, v4) in enumerate(zip(fts, v4s)):
        after = tokens[j - 2:j - 1] if j >= 2 else [norms]
        v2 = permuted(pick(low_pair, ft, v4, after), "blocks", swap2)
        vx = permuted(v2, "blocks", swap1)
        vy = permuted(pick(low_core, ft, v4, []), "blocks", swap1)
        out, token = distance_chunk(bit, own, norms, v4, v2, vx, vy, out, start)
        tokens.append(token)
        start += ft.shape[1]
    return out


def solution(mesh):
    in_specs = (P("blocks", None, "parts"), P(), P())
    out_specs = P(None, ("parts", "blocks"), None)
    return jax.shard_map(shards, mesh=mesh, in_specs=in_specs, out_specs=out_specs, check_vma=False)
```

```python
import functools
import math

import jax
import jax.numpy as jnp
from jax import lax
from jax.experimental import pallas as pl
from jax.experimental.pallas import tpu as pltpu
from jax.sharding import PartitionSpec as P


ROUNDS = 4
VMEM_BYTES = 58 * 1024 * 1024
UNIT = 1.0 / 512.0
BAD = -32768


def permuted(shard, axis, to):
    count = lax.axis_size(axis)
    return lax.ppermute(shard, axis, [(i, to(i, count)) for i in range(count)])


def shift4(i, count):
    return (i + 4) % count


def swap1(i, count):
    return i ^ 1


def swap2(i, count):
    return i ^ 2


def largest_divisor(value, limit):
    return max(d for d in range(1, limit + 1) if value % d == 0)


def features_kernel(slots_ref, x_ref, *refs, steps, tile, pitch, starts, unit):
    *ft_refs, atoms_ref, squares_ref = refs
    step = pl.program_id(0)
    per_step, _, rows, frames = x_ref.shape
    lanes = frames // 8

    @pl.when(step < steps)
    def _():
        def regroup(g, carry):
            for component in range(3):
                x = x_ref[g, component]
                if x.dtype != jnp.float32:
                    x = x.astype(jnp.int32).astype(jnp.float32)
                for top in range(0, rows, 8):
                    for s in range(8):
                        start = ((step * per_step + g) * rows + top) * 24 + component * 8 + s
                        atoms_ref[pl.ds(start, 8, stride=24), :] = x[
                            top:top + 8, s * lanes:(s + 1) * lanes]
            return carry

        lax.fori_loop(0, per_step, regroup, 0)

    @pl.when(step >= steps)
    def _():
        base = (step - steps) * tile
        unroll = 16

        def contacts(i, carry):
            for u in range(unroll):
                c = i * unroll + u
                first = slots_ref[0, base + c]
                second = slots_ref[1, base + c]
                squared = None
                for row in (0, 8, 16):
                    offset = (atoms_ref[pl.ds(pl.multiple_of(first + row, 8), 8), :]
                              - atoms_ref[pl.ds(pl.multiple_of(second + row, 8), 8), :])
                    squared = offset * offset if squared is None else squared + offset * offset
                squares_ref[pl.ds(c, 8, stride=pitch), :] = squared
            return carry

        lax.fori_loop(0, tile // unroll, contacts, 0)
        for ft_ref, start in zip(ft_refs, starts):
            for left in range(0, ft_ref.shape[1], lanes):
                s = (start + left) // lanes
                squared = squares_ref[s * pitch:s * pitch + tile, :] * (unit * unit) + 0.01
                squared = jnp.minimum(squared, 1e30)
                separation = squared * lax.rsqrt(squared)
                scale = math.log2(math.e) / 1.5
                feature = 1.0 / (1.0 + jnp.exp2(separation * scale - 8.0 * scale))
                ft_ref[:, left:left + lanes] = feature.astype(jnp.bfloat16)


def features_of(x, slots24, starts, widths, unit):
    groups, _, rows, frames = x.shape
    contacts = slots24.shape[1]
    per_step = largest_divisor(groups, max(1, 160 // rows))
    steps = groups // per_step
    tile = 512
    pitch = tile + 8
    return pl.pallas_call(
        functools.partial(features_kernel, steps=steps, tile=tile, pitch=pitch,
                          starts=starts, unit=unit),
        grid_spec=pltpu.PrefetchScalarGridSpec(
            num_scalar_prefetch=1,
            grid=(steps + contacts // tile,),
            in_specs=[pl.BlockSpec((per_step, 3, rows, frames),
                                   lambda i, s: (jnp.minimum(i, steps - 1), 0, 0, 0))],
            out_specs=[pl.BlockSpec((tile, width), lambda i, s: (jnp.maximum(i - steps, 0), 0))
                       for width in widths],
            scratch_shapes=[
                pltpu.VMEM((groups * rows * 24, frames // 8), jnp.float32),
                pltpu.VMEM((8 * pitch, frames // 8), jnp.float32),
            ],
        ),
        out_shape=[jax.ShapeDtypeStruct((contacts, width), jnp.bfloat16) for width in widths],
        compiler_params=pltpu.CompilerParams(vmem_limit_bytes=VMEM_BYTES),
        name="features",
    )(slots24, x)


def own_kernel(*refs, starts):
    *ft_refs, f_ref, norm_ref = refs

    @pl.when(pl.program_id(0) == 0)
    def _():
        norm_ref[...] = jnp.zeros_like(norm_ref)

    for ft_ref, row in zip(ft_refs, starts):
        width = ft_ref.shape[1]
        own = ft_ref[...].astype(jnp.float32).T
        f_ref[row:row + width, :] = own.astype(jnp.bfloat16)
        norm_ref[row:row + width, :] += jnp.sum(own * own, axis=1, keepdims=True)


def own_features(fts, starts):
    contacts = fts[0].shape[0]
    frames = sum(ft.shape[1] for ft in fts)
    tile = 512
    return pl.pallas_call(
        functools.partial(own_kernel, starts=starts),
        grid=(contacts // tile,),
        in_specs=[pl.BlockSpec((tile, ft.shape[1]), lambda i: (i, 0)) for ft in fts],
        out_specs=[
            pl.BlockSpec((frames, tile), lambda i: (0, i)),
            pl.BlockSpec((frames, 1), lambda i: (0, 0)),
        ],
        out_shape=[
            jax.ShapeDtypeStruct((frames, contacts), jnp.bfloat16),
            jax.ShapeDtypeStruct((frames, 1), jnp.float32),
        ],
        compiler_params=pltpu.CompilerParams(vmem_limit_bytes=VMEM_BYTES),
        name="own_features",
    )(*fts)


def pick_kernel(flag_ref, first_ref, second_ref, *refs):
    out_ref, rows_ref, in_sems, out_sems = refs[-4:]
    parts = in_sems.shape[0]
    size = rows_ref.shape[0] // parts
    spans = [pl.ds(k * size, size) for k in range(parts)]

    def fetch(source_ref):
        for k, span in enumerate(spans):
            pltpu.make_async_copy(source_ref.at[span], rows_ref.at[span], in_sems.at[k]).start()

    @pl.when(flag_ref[0] == 1)
    def _():
        fetch(first_ref)

    @pl.when(flag_ref[0] != 1)
    def _():
        fetch(second_ref)

    for k, span in enumerate(spans):
        pltpu.make_async_copy(first_ref.at[span], rows_ref.at[span], in_sems.at[k]).wait()
        pltpu.make_async_copy(rows_ref.at[span], out_ref.at[span], out_sems.at[k]).start()
    for k, span in enumerate(spans):
        pltpu.make_async_copy(rows_ref.at[span], out_ref.at[span], out_sems.at[k]).wait()


def pick(flag, first, second, after):
    anywhere = pl.BlockSpec(memory_space=pl.ANY)
    return pl.pallas_call(
        pick_kernel,
        in_specs=[pl.BlockSpec(memory_space=pltpu.SMEM)] + [anywhere] * (2 + len(after)),
        out_specs=anywhere,
        out_shape=jax.ShapeDtypeStruct(first.shape, first.dtype),
        scratch_shapes=[pltpu.VMEM(first.shape, first.dtype), pltpu.SemaphoreType.DMA((4,)),
                        pltpu.SemaphoreType.DMA((4,))],
        name="pick",
    )(flag, first, second, *after)


def distance_kernel(bit_ref, own_ref, norm_ref, v4_ref, v2_ref, vx_ref, vy_ref, *refs, aliased):
    refs = refs[1:] if aliased else refs
    out_ref, token_ref, vnorm_ref = refs

    @pl.when(pl.program_id(0) == 0)
    def _():
        for r, ref in enumerate((vx_ref, v2_ref, vy_ref, v4_ref)):
            wide = ref[...].astype(jnp.float32)
            vnorm_ref[r, 0:1, :] = jnp.sum(wide * wide, axis=0, keepdims=True)
        token_ref[...] = jnp.zeros_like(token_ref)

    def rounds(places):
        for r, ref in enumerate((vx_ref, v2_ref, vy_ref, v4_ref)):
            inter = jnp.dot(own_ref[...], ref[...], preferred_element_type=jnp.float32)
            ratio = inter / (norm_ref[...] + vnorm_ref[r, 0:1, :] - inter + 1e-06)
            out_ref[places[r]] = (1.0 - ratio).astype(jnp.bfloat16)

    @pl.when(bit_ref[0] == 1)
    def _():
        rounds((2, 1, 0, 3))

    @pl.when(bit_ref[0] != 1)
    def _():
        rounds((0, 1, 2, 3))


def distance_chunk(bit, own, norms, v4, v2, vx, vy, out, start):
    frames, contacts = own.shape
    width = v4.shape[1]
    tile = 256
    block = start // width
    aliased = out is not None
    in_specs = [
        pl.BlockSpec(memory_space=pltpu.SMEM),
        pl.BlockSpec((tile, contacts), lambda i: (i, 0)),
        pl.BlockSpec((tile, 1), lambda i: (i, 0)),
    ] + [pl.BlockSpec((contacts, width), lambda i: (0, 0))] * 4
    args = [bit, own, norms, v4, v2, vx, vy]
    if aliased:
        in_specs.append(pl.BlockSpec(memory_space=pl.ANY))
        args.append(out)
    return pl.pallas_call(
        functools.partial(distance_kernel, aliased=aliased),
        grid=(frames // tile,),
        in_specs=in_specs,
        out_specs=[
            pl.BlockSpec((ROUNDS, tile, width), lambda i: (0, i, block)),
            pl.BlockSpec((8, 128), lambda i: (0, 0)),
        ],
        out_shape=[
            jax.ShapeDtypeStruct((ROUNDS, frames, frames), jnp.bfloat16),
            jax.ShapeDtypeStruct((8, 128), jnp.float32),
        ],
        scratch_shapes=[pltpu.VMEM((ROUNDS, 8, width), jnp.float32)],
        input_output_aliases={7: 0} if aliased else {},
        compiler_params=pltpu.CompilerParams(vmem_limit_bytes=VMEM_BYTES),
    )(*args)


def contact_slots(pairs, res_slot):
    hits = pairs[:, :, None] == res_slot[None, None, :]
    places = jnp.arange(res_slot.shape[0], dtype=jnp.int32)
    return jnp.sum(jnp.where(hits, places, 0), axis=2, dtype=jnp.int32)


def split_kernel(x_ref, pieces_ref, extent_ref, spread_ref):
    step = pl.program_id(0)
    _, _, _, frames = pieces_ref.shape
    per_step = x_ref.shape[2] // frames

    @pl.when(step == 0)
    def _():
        extent_ref[...] = jnp.zeros_like(extent_ref)
        spread_ref[...] = jnp.full_like(spread_ref, jnp.inf)

    for k in range(per_step):
        x = x_ref[:, :, k * frames:(k + 1) * frames]
        coded = jnp.clip(jnp.round(x * (1.0 / UNIT)), -32767.0, 32767.0)
        pieces_ref[step * per_step + k] = coded.astype(jnp.int32).astype(jnp.int16)
        extent_ref[...] = jnp.maximum(extent_ref[...], jnp.max(jnp.abs(x), axis=0))
        mean = jnp.sum(x, axis=2, keepdims=True) * (1.0 / frames)
        square = jnp.sum(x * x, axis=2, keepdims=True) * (1.0 / frames)
        spread = jnp.mean(square - mean * mean, axis=(0, 1), keepdims=True)[0]
        spread_ref[...] = jnp.minimum(spread_ref[...], spread)

    @pl.when(step == pl.num_programs(0) - 1)
    def _():
        fine = (jnp.max(extent_ref[...]) <= 32767.0 * UNIT) & (jnp.min(spread_ref[...]) >= 0.05)

        @pl.when(jnp.logical_not(fine))
        def _():
            pieces_ref[...] = jnp.full(pieces_ref.shape, BAD, jnp.int32).astype(jnp.int16)


def split_blocks(coords, count):
    _, rows, frames = coords.shape
    per_block = frames // count
    per_step = 2 if count % 2 == 0 else 1
    return pl.pallas_call(
        split_kernel,
        grid=(count // per_step,),
        in_specs=[pl.BlockSpec((3, rows, per_step * per_block), lambda i: (0, 0, i))],
        out_specs=pl.BlockSpec((count, 3, rows, per_block), lambda i: (0, 0, 0, 0)),
        out_shape=jax.ShapeDtypeStruct((count, 3, rows, per_block), jnp.int16),
        scratch_shapes=[pltpu.VMEM((rows, per_block), jnp.float32), pltpu.VMEM((1, 1), jnp.float32)],
        compiler_params=pltpu.CompilerParams(vmem_limit_bytes=VMEM_BYTES),
        name="split_blocks",
    )(coords)


def exchanged(pieces):
    got = lax.all_to_all(pieces, "blocks", split_axis=0, concat_axis=0, tiled=True)
    count, _, rows, per_block = got.shape
    if rows % 8:
        got = got.transpose(0, 2, 1, 3).reshape(count * rows // 8, 8, 3, per_block)
        got = got.transpose(0, 2, 1, 3)
    return got


def contact_features(coords, slots24, starts, widths):
    count = lax.axis_size("blocks")
    narrow = exchanged(split_blocks(coords.transpose(1, 0, 2), count))
    all_fine = jnp.all(narrow[:, 0, 0, 0] != BAD)

    def coarse():
        return features_of(narrow, slots24, starts, widths, UNIT)

    def exact():
        pieces = coords.reshape(coords.shape[0], 3, count, -1).transpose(2, 1, 0, 3)
        return features_of(exchanged(pieces), slots24, starts, widths, 1.0)

    return lax.cond(all_fine, coarse, exact)


def shards(coords, pairs, res_slot):
    index = lax.axis_index("blocks")
    lanes = coords.shape[2] // lax.axis_size("blocks") // 8
    widths = [lanes * n for n in (1, 2, 2, 2, 1)]
    starts = [lanes * n for n in (0, 2, 4, 6, 1)]

    slots24 = contact_slots(pairs, res_slot) * 24
    fts = contact_features(coords, slots24, starts, widths)

    bit = (index & 1).astype(jnp.int32).reshape(1)
    low_core = 1 - bit
    low_pair = 1 - ((index >> 1) & 1).astype(jnp.int32).reshape(1)

    v4s = []
    for ft in fts:
        v4s.append(permuted(ft, "blocks", shift4))
    own, norms = own_features(fts, starts)

    out = None
    tokens = []
    for j, (ft, v4) in enumerate(zip(fts, v4s)):
        after = tokens[j - 2:j - 1] if j >= 2 else [norms]
        sent = pick(low_pair, ft, v4, after)
        v2 = permuted(sent, "blocks", swap2)
        sent = pick(low_core, ft, v4, [])
        vy = permuted(sent, "blocks", swap1)
        vx = permuted(v2, "blocks", swap1)
        out, token = distance_chunk(bit, own, norms, v4, v2, vx, vy, out, starts[j])
        tokens.append(token)
    return out


def solution(mesh):
    in_specs = (P("blocks", None, "parts"), P(), P())
    out_specs = P(None, ("parts", "blocks"), None)
    return jax.shard_map(shards, mesh=mesh, in_specs=in_specs, out_specs=out_specs, check_vma=False)
```

```python
import functools
import math

import jax
import jax.numpy as jnp
from jax import lax
from jax.experimental import pallas as pl
from jax.experimental.pallas import tpu as pltpu
from jax.sharding import PartitionSpec as P


ROUNDS = 4
VMEM_BYTES = 24 * 1024 * 1024
UNIT = 1.0 / 512.0
BAD = -32768


def permuted(shard, axis, to):
    count = lax.axis_size(axis)
    return lax.ppermute(shard, axis, [(i, to(i, count)) for i in range(count)])


def shift4(i, count):
    return (i + 4) % count


def swap1(i, count):
    return i ^ 1


def swap2(i, count):
    return i ^ 2


def largest_divisor(value, limit):
    return max(d for d in range(1, limit + 1) if value % d == 0)


def features_kernel(slots_ref, x_ref, *refs, steps, tile, pitch, starts, unit):
    *ft_refs, atoms_ref, squares_ref = refs
    step = pl.program_id(0)
    per_step, _, rows, frames = x_ref.shape
    lanes = frames // 8

    @pl.when(step < steps)
    def _():
        def regroup(g, carry):
            for component in range(3):
                x = x_ref[g, component]
                if x.dtype != jnp.float32:
                    x = x.astype(jnp.int32).astype(jnp.float32)
                for top in range(0, rows, 8):
                    for s in range(8):
                        start = ((step * per_step + g) * rows + top) * 24 + component * 8 + s
                        atoms_ref[pl.ds(start, 8, stride=24), :] = x[
                            top:top + 8, s * lanes:(s + 1) * lanes]
            return carry

        lax.fori_loop(0, per_step, regroup, 0)

    @pl.when(step >= steps)
    def _():
        base = (step - steps) * tile
        unroll = 16

        def contacts(i, carry):
            for u in range(unroll):
                c = i * unroll + u
                first = slots_ref[0, base + c]
                second = slots_ref[1, base + c]
                squared = None
                for row in (0, 8, 16):
                    offset = (atoms_ref[pl.ds(pl.multiple_of(first + row, 8), 8), :]
                              - atoms_ref[pl.ds(pl.multiple_of(second + row, 8), 8), :])
                    squared = offset * offset if squared is None else squared + offset * offset
                squares_ref[pl.ds(c, 8, stride=pitch), :] = squared
            return carry

        lax.fori_loop(0, tile // unroll, contacts, 0)
        for ft_ref, start in zip(ft_refs, starts):
            for left in range(0, ft_ref.shape[1], lanes):
                s = (start + left) // lanes
                squared = squares_ref[s * pitch:s * pitch + tile, :] * (unit * unit) + 0.01
                squared = jnp.minimum(squared, 1e30)
                separation = squared * lax.rsqrt(squared)
                scale = math.log2(math.e) / 1.5
                feature = 1.0 / (1.0 + jnp.exp2(separation * scale - 8.0 * scale))
                ft_ref[:, left:left + lanes] = feature.astype(jnp.bfloat16)


def features_of(x, slots24, starts, widths, unit):
    groups, _, rows, frames = x.shape
    contacts = slots24.shape[1]
    per_step = largest_divisor(groups, max(1, 160 // rows))
    steps = groups // per_step
    tile = 512
    pitch = tile + 8
    return pl.pallas_call(
        functools.partial(features_kernel, steps=steps, tile=tile, pitch=pitch,
                          starts=starts, unit=unit),
        grid_spec=pltpu.PrefetchScalarGridSpec(
            num_scalar_prefetch=1,
            grid=(steps + contacts // tile,),
            in_specs=[pl.BlockSpec((per_step, 3, rows, frames),
                                   lambda i, s: (jnp.minimum(i, steps - 1), 0, 0, 0))],
            out_specs=[pl.BlockSpec((tile, width), lambda i, s: (jnp.maximum(i - steps, 0), 0))
                       for width in widths],
            scratch_shapes=[
                pltpu.VMEM((groups * rows * 24, frames // 8), jnp.float32),
                pltpu.VMEM((8 * pitch, frames // 8), jnp.float32),
            ],
        ),
        out_shape=[jax.ShapeDtypeStruct((contacts, width), jnp.bfloat16) for width in widths],
        compiler_params=pltpu.CompilerParams(vmem_limit_bytes=VMEM_BYTES),
        name="features",
    )(slots24, x)


def own_kernel(*refs, starts):
    *ft_refs, f_ref, norm_ref = refs

    @pl.when(pl.program_id(0) == 0)
    def _():
        norm_ref[...] = jnp.zeros_like(norm_ref)

    for ft_ref, row in zip(ft_refs, starts):
        width = ft_ref.shape[1]
        own = ft_ref[...].astype(jnp.float32).T
        f_ref[row:row + width, :] = own.astype(jnp.bfloat16)
        norm_ref[row:row + width, :] += jnp.sum(own * own, axis=1, keepdims=True)


def own_features(fts, starts):
    contacts = fts[0].shape[0]
    frames = sum(ft.shape[1] for ft in fts)
    tile = 512
    return pl.pallas_call(
        functools.partial(own_kernel, starts=starts),
        grid=(contacts // tile,),
        in_specs=[pl.BlockSpec((tile, ft.shape[1]), lambda i: (i, 0)) for ft in fts],
        out_specs=[
            pl.BlockSpec((frames, tile), lambda i: (0, i)),
            pl.BlockSpec((frames, 1), lambda i: (0, 0)),
        ],
        out_shape=[
            jax.ShapeDtypeStruct((frames, contacts), jnp.bfloat16),
            jax.ShapeDtypeStruct((frames, 1), jnp.float32),
        ],
        compiler_params=pltpu.CompilerParams(vmem_limit_bytes=VMEM_BYTES),
        name="own_features",
    )(*fts)


def pick_kernel(flag_ref, first_ref, second_ref, *refs):
    out_ref, rows_ref, in_sems, out_sems = refs[-4:]
    parts = in_sems.shape[0]
    size = rows_ref.shape[0] // parts
    spans = [pl.ds(k * size, size) for k in range(parts)]

    def fetch(source_ref):
        for k, span in enumerate(spans):
            pltpu.make_async_copy(source_ref.at[span], rows_ref.at[span], in_sems.at[k]).start()

    @pl.when(flag_ref[0] == 1)
    def _():
        fetch(first_ref)

    @pl.when(flag_ref[0] != 1)
    def _():
        fetch(second_ref)

    for k, span in enumerate(spans):
        pltpu.make_async_copy(first_ref.at[span], rows_ref.at[span], in_sems.at[k]).wait()
        pltpu.make_async_copy(rows_ref.at[span], out_ref.at[span], out_sems.at[k]).start()
    for k, span in enumerate(spans):
        pltpu.make_async_copy(rows_ref.at[span], out_ref.at[span], out_sems.at[k]).wait()


def pick(flag, first, second, after):
    anywhere = pl.BlockSpec(memory_space=pl.ANY)
    return pl.pallas_call(
        pick_kernel,
        in_specs=[pl.BlockSpec(memory_space=pltpu.SMEM)] + [anywhere] * (2 + len(after)),
        out_specs=anywhere,
        out_shape=jax.ShapeDtypeStruct(first.shape, first.dtype),
        scratch_shapes=[pltpu.VMEM(first.shape, first.dtype), pltpu.SemaphoreType.DMA((4,)),
                        pltpu.SemaphoreType.DMA((4,))],
        compiler_params=pltpu.CompilerParams(vmem_limit_bytes=VMEM_BYTES // 4),
        name="pick",
    )(flag, first, second, *after)


def distance_kernel(bit_ref, own_ref, norm_ref, v4_ref, v2_ref, vx_ref, vy_ref, *refs, aliased):
    refs = refs[1:] if aliased else refs
    out_ref, token_ref, vnorm_ref = refs

    @pl.when(pl.program_id(0) == 0)
    def _():
        for r, ref in enumerate((vx_ref, v2_ref, vy_ref, v4_ref)):
            wide = ref[...].astype(jnp.float32)
            vnorm_ref[r, 0:1, :] = jnp.sum(wide * wide, axis=0, keepdims=True)
        token_ref[...] = jnp.zeros_like(token_ref)

    def rounds(places):
        for r, ref in enumerate((vx_ref, v2_ref, vy_ref, v4_ref)):
            inter = jnp.dot(own_ref[...], ref[...], preferred_element_type=jnp.float32)
            ratio = inter / (norm_ref[...] + vnorm_ref[r, 0:1, :] - inter + 1e-06)
            out_ref[places[r]] = (1.0 - ratio).astype(jnp.bfloat16)

    @pl.when(bit_ref[0] == 1)
    def _():
        rounds((2, 1, 0, 3))

    @pl.when(bit_ref[0] != 1)
    def _():
        rounds((0, 1, 2, 3))


def distance_chunk(bit, own, norms, v4, v2, vx, vy, out, start):
    frames, contacts = own.shape
    width = v4.shape[1]
    tile = 256
    block = start // width
    aliased = out is not None
    in_specs = [
        pl.BlockSpec(memory_space=pltpu.SMEM),
        pl.BlockSpec((tile, contacts), lambda i: (i, 0)),
        pl.BlockSpec((tile, 1), lambda i: (i, 0)),
    ] + [pl.BlockSpec((contacts, width), lambda i: (0, 0))] * 4
    args = [bit, own, norms, v4, v2, vx, vy]
    if aliased:
        in_specs.append(pl.BlockSpec(memory_space=pl.ANY))
        args.append(out)
    return pl.pallas_call(
        functools.partial(distance_kernel, aliased=aliased),
        grid=(frames // tile,),
        in_specs=in_specs,
        out_specs=[
            pl.BlockSpec((ROUNDS, tile, width), lambda i: (0, i, block)),
            pl.BlockSpec((8, 128), lambda i: (0, 0)),
        ],
        out_shape=[
            jax.ShapeDtypeStruct((ROUNDS, frames, frames), jnp.bfloat16),
            jax.ShapeDtypeStruct((8, 128), jnp.float32),
        ],
        scratch_shapes=[pltpu.VMEM((ROUNDS, 8, width), jnp.float32)],
        input_output_aliases={7: 0} if aliased else {},
        compiler_params=pltpu.CompilerParams(vmem_limit_bytes=VMEM_BYTES),
    )(*args)


def half_kernel(places_ref, own_ref, norm_ref, first_ref, second_ref, *refs, aliased):
    refs = refs[1:] if aliased else refs
    out_ref, token_ref, vnorm_ref = refs
    token_ref[...] = jnp.zeros_like(token_ref)
    for which, ref in enumerate((first_ref, second_ref)):
        @pl.when(pl.program_id(0) == which)
        def _():
            @pl.when(pl.program_id(1) == 0)
            def _():
                wide = ref[...].astype(jnp.float32)
                vnorm_ref[0:1, :] = jnp.sum(wide * wide, axis=0, keepdims=True)

            inter = jnp.dot(own_ref[...], ref[...], preferred_element_type=jnp.float32)
            ratio = inter / (norm_ref[...] + vnorm_ref[0:1, :] - inter + 1e-06)
            out_ref[0] = (1.0 - ratio).astype(jnp.bfloat16)


def distance_half(places, own, norms, first, second, out, start):
    frames, contacts = own.shape
    width = first.shape[1]
    tile = 512
    block = start // width
    aliased = out is not None
    in_specs = [
        pl.BlockSpec((tile, contacts), lambda r, i, p: (i, 0)),
        pl.BlockSpec((tile, 1), lambda r, i, p: (i, 0)),
    ] + [pl.BlockSpec((contacts, width), lambda r, i, p: (0, 0))] * 2
    args = [own, norms, first, second]
    if aliased:
        in_specs.append(pl.BlockSpec(memory_space=pl.ANY))
        args.append(out)
    return pl.pallas_call(
        functools.partial(half_kernel, aliased=aliased),
        grid_spec=pltpu.PrefetchScalarGridSpec(
            num_scalar_prefetch=1,
            grid=(2, frames // tile),
            in_specs=in_specs,
            out_specs=[
                pl.BlockSpec((1, tile, width), lambda r, i, p: (p[r], i, block)),
                pl.BlockSpec((8, 128), lambda r, i, p: (0, 0)),
            ],
            scratch_shapes=[pltpu.VMEM((8, width), jnp.float32)],
        ),
        out_shape=[
            jax.ShapeDtypeStruct((ROUNDS, frames, frames), jnp.bfloat16),
            jax.ShapeDtypeStruct((8, 128), jnp.float32),
        ],
        input_output_aliases={5: 0} if aliased else {},
        compiler_params=pltpu.CompilerParams(vmem_limit_bytes=VMEM_BYTES),
    )(places, *args)


def contact_slots(pairs, res_slot):
    hits = pairs[:, :, None] == res_slot[None, None, :]
    places = jnp.arange(res_slot.shape[0], dtype=jnp.int32)
    return jnp.sum(jnp.where(hits, places, 0), axis=2, dtype=jnp.int32)


def split_kernel(x_ref, pieces_ref, extent_ref, spread_ref):
    step = pl.program_id(0)
    _, _, _, frames = pieces_ref.shape
    per_step = x_ref.shape[2] // frames

    @pl.when(step == 0)
    def _():
        extent_ref[...] = jnp.zeros_like(extent_ref)
        spread_ref[...] = jnp.full_like(spread_ref, jnp.inf)

    for k in range(per_step):
        x = x_ref[:, :, k * frames:(k + 1) * frames]
        coded = jnp.clip(jnp.round(x * (1.0 / UNIT)), -32767.0, 32767.0)
        pieces_ref[step * per_step + k] = coded.astype(jnp.int32).astype(jnp.int16)
        extent_ref[...] = jnp.maximum(extent_ref[...], jnp.max(jnp.abs(x), axis=0))
        mean = jnp.sum(x, axis=2, keepdims=True) * (1.0 / frames)
        square = jnp.sum(x * x, axis=2, keepdims=True) * (1.0 / frames)
        spread = jnp.mean(square - mean * mean, axis=(0, 1), keepdims=True)[0]
        spread_ref[...] = jnp.minimum(spread_ref[...], spread)

    @pl.when(step == pl.num_programs(0) - 1)
    def _():
        fine = (jnp.max(extent_ref[...]) <= 32767.0 * UNIT) & (jnp.min(spread_ref[...]) >= 0.05)

        @pl.when(jnp.logical_not(fine))
        def _():
            pieces_ref[...] = jnp.full(pieces_ref.shape, BAD, jnp.int32).astype(jnp.int16)


def split_blocks(coords, count):
    _, rows, frames = coords.shape
    per_block = frames // count
    per_step = largest_divisor(count, 4)
    return pl.pallas_call(
        split_kernel,
        grid=(count // per_step,),
        in_specs=[pl.BlockSpec((3, rows, per_step * per_block), lambda i: (0, 0, i))],
        out_specs=pl.BlockSpec((count, 3, rows, per_block), lambda i: (0, 0, 0, 0)),
        out_shape=jax.ShapeDtypeStruct((count, 3, rows, per_block), jnp.int16),
        scratch_shapes=[pltpu.VMEM((rows, per_block), jnp.float32), pltpu.VMEM((1, 1), jnp.float32)],
        compiler_params=pltpu.CompilerParams(vmem_limit_bytes=58 * 1024 * 1024),
        name="split_blocks",
    )(coords)


def exchanged(pieces):
    got = lax.all_to_all(pieces, "blocks", split_axis=0, concat_axis=0, tiled=True)
    count, _, rows, per_block = got.shape
    if rows % 8:
        got = got.transpose(0, 2, 1, 3).reshape(count * rows // 8, 8, 3, per_block)
        got = got.transpose(0, 2, 1, 3)
    return got


def contact_features(coords, slots24, starts, widths):
    count = lax.axis_size("blocks")
    narrow = exchanged(split_blocks(coords.transpose(1, 0, 2), count))
    all_fine = jnp.all(narrow[:, 0, 0, 0] != BAD)

    def coarse():
        return features_of(narrow, slots24, starts, widths, UNIT)

    def exact():
        pieces = coords.reshape(coords.shape[0], 3, count, -1).transpose(2, 1, 0, 3)
        return features_of(exchanged(pieces), slots24, starts, widths, 1.0)

    return lax.cond(all_fine, coarse, exact)


def shards(coords, pairs, res_slot):
    index = lax.axis_index("blocks")
    lanes = coords.shape[2] // lax.axis_size("blocks") // 8
    widths = [lanes * n for n in (1, 1, 2, 2, 2)]
    starts = [lanes * n for n in (0, 1, 2, 4, 6)]

    slots24 = contact_slots(pairs, res_slot) * 24
    fts = contact_features(coords, slots24, starts, widths)

    bit = (index & 1).astype(jnp.int32).reshape(1)
    low_core = 1 - bit
    low_pair = 1 - ((index >> 1) & 1).astype(jnp.int32).reshape(1)

    v4s = []
    for ft in fts:
        v4s.append(permuted(ft, "blocks", shift4))
    own, norms = own_features(fts, starts)

    out = None
    tokens = []
    for j, (ft, v4) in enumerate(zip(fts, v4s)):
        after = tokens[j - 2:j - 1] if j >= 2 else [norms]
        sent = pick(low_pair, ft, v4, after)
        v2 = permuted(sent, "blocks", swap2)
        sent = pick(low_core, ft, v4, [])
        vy = permuted(sent, "blocks", swap1)
        vx = permuted(v2, "blocks", swap1)
        if j + 1 < len(fts):
            out, token = distance_chunk(bit, own, norms, v4, v2, vx, vy, out, starts[j])
        else:
            three = jnp.full((1,), 3, jnp.int32)
            one = jnp.full((1,), 1, jnp.int32)
            places = jnp.concatenate([three, 2 - 2 * bit])
            out, token = distance_half(places, own, norms, v4, vy, out, starts[j])
            places = jnp.concatenate([one, 2 * bit])
            out, token = distance_half(places, own, norms, v2, vx, out, starts[j])
        tokens.append(token)
    return out


def solution(mesh):
    in_specs = (P("blocks", None, "parts"), P(), P())
    out_specs = P(None, ("parts", "blocks"), None)
    return jax.shard_map(shards, mesh=mesh, in_specs=in_specs, out_specs=out_specs, check_vma=False)
```

```python
import functools
import math

import jax
import jax.numpy as jnp
from jax import lax
from jax.experimental import pallas as pl
from jax.experimental.pallas import tpu as pltpu
from jax.sharding import PartitionSpec as P


ROUNDS = 4
CHUNKS = 8
VMEM_BYTES = 24 * 1024 * 1024
UNIT = 1.0 / 512.0
BAD = -32768


def permuted(shard, axis, to):
    count = lax.axis_size(axis)
    return lax.ppermute(shard, axis, [(i, to(i, count)) for i in range(count)])


def shift4(i, count):
    return (i + 4) % count


def swap1(i, count):
    return i ^ 1


def swap2(i, count):
    return i ^ 2


def largest_divisor(value, limit):
    return max(d for d in range(1, limit + 1) if value % d == 0)


def features_kernel(slots_ref, x_ref, *refs, steps, tile, pitch, starts, unit):
    *ft_refs, atoms_ref, squares_ref = refs
    step = pl.program_id(0)
    per_step, _, rows, frames = x_ref.shape
    lanes = frames // 8

    @pl.when(step < steps)
    def _():
        def regroup(g, carry):
            for component in range(3):
                x = x_ref[g, component]
                if x.dtype != jnp.float32:
                    x = x.astype(jnp.int32).astype(jnp.float32)
                for top in range(0, rows, 8):
                    for s in range(8):
                        start = ((step * per_step + g) * rows + top) * 24 + component * 8 + s
                        atoms_ref[pl.ds(start, 8, stride=24), :] = x[
                            top:top + 8, s * lanes:(s + 1) * lanes]
            return carry

        lax.fori_loop(0, per_step, regroup, 0)

    @pl.when(step >= steps)
    def _():
        unroll = 32
        count = slots_ref.shape[0] // 2

        def contacts(i, carry):
            base = (step - steps) * tile + i * unroll
            for u in range(unroll):
                c = i * unroll + u
                first = slots_ref[base + u]
                second = slots_ref[base + u + count]
                squared = None
                for row in (0, 8, 16):
                    offset = (atoms_ref[pl.ds(pl.multiple_of(first + row, 8), 8), :]
                              - atoms_ref[pl.ds(pl.multiple_of(second + row, 8), 8), :])
                    squared = offset * offset if squared is None else squared + offset * offset
                squares_ref[pl.ds(c, 8, stride=pitch), :] = squared
            return carry

        lax.fori_loop(0, tile // unroll, contacts, 0)
        for ft_ref, start in zip(ft_refs, starts):
            for left in range(0, ft_ref.shape[1], lanes):
                s = (start + left) // lanes
                squared = squares_ref[s * pitch:s * pitch + tile, :] * (unit * unit) + 0.01
                squared = jnp.minimum(squared, 1e30)
                separation = squared * lax.rsqrt(squared)
                scale = math.log2(math.e) / 1.5
                feature = 1.0 / (1.0 + jnp.exp2(separation * scale - 8.0 * scale))
                ft_ref[:, left:left + lanes] = feature.astype(jnp.bfloat16)


def features_of(x, slots24, starts, widths, unit):
    groups, _, rows, frames = x.shape
    contacts = slots24.shape[0] // 2
    per_step = largest_divisor(groups, max(1, 160 // rows))
    steps = groups // per_step
    tile = 512
    pitch = tile + 8
    return pl.pallas_call(
        functools.partial(features_kernel, steps=steps, tile=tile, pitch=pitch,
                          starts=starts, unit=unit),
        grid_spec=pltpu.PrefetchScalarGridSpec(
            num_scalar_prefetch=1,
            grid=(steps + contacts // tile,),
            in_specs=[pl.BlockSpec((per_step, 3, rows, frames),
                                   lambda i, s: (jnp.minimum(i, steps - 1), 0, 0, 0))],
            out_specs=[pl.BlockSpec((tile, width), lambda i, s: (jnp.maximum(i - steps, 0), 0))
                       for width in widths],
            scratch_shapes=[
                pltpu.VMEM((groups * rows * 24, frames // 8), jnp.float32),
                pltpu.VMEM((8 * pitch, frames // 8), jnp.float32),
            ],
        ),
        out_shape=[jax.ShapeDtypeStruct((contacts, width), jnp.bfloat16) for width in widths],
        compiler_params=pltpu.CompilerParams(vmem_limit_bytes=VMEM_BYTES),
        name="features",
    )(slots24, x)


def own_kernel(*refs, starts):
    *ft_refs, f_ref, norm_ref = refs

    @pl.when(pl.program_id(0) == 0)
    def _():
        norm_ref[...] = jnp.zeros_like(norm_ref)

    for ft_ref, row in zip(ft_refs, starts):
        width = ft_ref.shape[1]
        own = ft_ref[...].astype(jnp.float32).T
        f_ref[row:row + width, :] = own.astype(jnp.bfloat16)
        norm_ref[row:row + width, :] += jnp.sum(own * own, axis=1, keepdims=True)


def own_features(fts, starts):
    contacts = fts[0].shape[0]
    frames = sum(ft.shape[1] for ft in fts)
    tile = 512
    return pl.pallas_call(
        functools.partial(own_kernel, starts=starts),
        grid=(contacts // tile,),
        in_specs=[pl.BlockSpec((tile, ft.shape[1]), lambda i: (i, 0)) for ft in fts],
        out_specs=[
            pl.BlockSpec((frames, tile), lambda i: (0, i)),
            pl.BlockSpec((frames, 1), lambda i: (0, 0)),
        ],
        out_shape=[
            jax.ShapeDtypeStruct((frames, contacts), jnp.bfloat16),
            jax.ShapeDtypeStruct((frames, 1), jnp.float32),
        ],
        compiler_params=pltpu.CompilerParams(vmem_limit_bytes=VMEM_BYTES),
        name="own_features",
    )(*fts)


def pick_kernel(flag_ref, *refs, count, rest):
    first_refs, second_refs = refs[:count], refs[count:2 * count]
    out_ref, rows_ref, in_sems, out_sems = refs[2 * count + rest:]
    parts = in_sems.shape[1]
    size = rows_ref.shape[1] // parts
    spans = [(n, k, pl.ds(k * size, size)) for n in range(count) for k in range(parts)]

    def fetch(source_refs):
        return [pltpu.make_async_copy(source_refs[n].at[span], rows_ref.at[n, span], in_sems.at[n, k])
                for n, k, span in spans]

    @pl.when(flag_ref[0] == 1)
    def _():
        for copy in fetch(first_refs):
            copy.start()

    @pl.when(flag_ref[0] != 1)
    def _():
        for copy in fetch(second_refs):
            copy.start()

    stores = [pltpu.make_async_copy(rows_ref.at[n, span], out_ref.at[n, span], out_sems.at[n, k])
              for n, k, span in spans]
    for copy, store in zip(fetch(first_refs), stores):
        copy.wait()
        store.start()
    for store in stores:
        store.wait()


def pick(flag, firsts, seconds, after):
    anywhere = pl.BlockSpec(memory_space=pl.ANY)
    count = len(firsts)
    shape = (count,) + firsts[0].shape
    return pl.pallas_call(
        functools.partial(pick_kernel, count=count, rest=len(after)),
        in_specs=[pl.BlockSpec(memory_space=pltpu.SMEM)] + [anywhere] * (2 * count + len(after)),
        out_specs=anywhere,
        out_shape=jax.ShapeDtypeStruct(shape, firsts[0].dtype),
        scratch_shapes=[pltpu.VMEM(shape, firsts[0].dtype), pltpu.SemaphoreType.DMA((count, 4)),
                        pltpu.SemaphoreType.DMA((count, 4))],
        compiler_params=pltpu.CompilerParams(vmem_limit_bytes=VMEM_BYTES // 4),
        name="pick",
    )(flag, *firsts, *seconds, *after)


def side_by_side(refs):
    return jnp.concatenate([ref[...].reshape(ref.shape[-2:]) for ref in refs], axis=1)


def block_specs(arrays):
    specs = []
    for array in arrays:
        zeros = (0,) * array.ndim
        specs.append(pl.BlockSpec(array.shape, lambda *ids, zeros=zeros: zeros))
    return specs


def tanimoto(own_ref, norm_ref, visitor, visitor_norm):
    inter = jnp.dot(own_ref[...], visitor, preferred_element_type=jnp.float32)
    ratio = inter / (norm_ref[...] + visitor_norm - inter + 1e-06)
    return (1.0 - ratio).astype(jnp.bfloat16)


def column_norms(features):
    wide = features.astype(jnp.float32)
    return jnp.sum(wide * wide, axis=0, keepdims=True)


def distance_kernel(bit_ref, own_ref, norm_ref, *refs, aliased):
    visitors = [refs[2 * r:2 * r + 2] for r in range(ROUNDS)]
    out_ref, token_ref, vnorm_ref = refs[2 * ROUNDS + (1 if aliased else 0):]

    @pl.when(pl.program_id(0) == 0)
    def _():
        for r, pair in enumerate(visitors):
            vnorm_ref[r, 0:1, :] = column_norms(side_by_side(pair))
        token_ref[...] = jnp.zeros_like(token_ref)

    def rounds(places):
        for r, pair in enumerate(visitors):
            out_ref[places[r]] = tanimoto(own_ref, norm_ref, side_by_side(pair), vnorm_ref[r, 0:1, :])

    @pl.when(bit_ref[0] == 1)
    def _():
        rounds((2, 1, 0, 3))

    @pl.when(bit_ref[0] != 1)
    def _():
        rounds((0, 1, 2, 3))


def distance_pair(bit, own, norms, vx, v2, vy, v4, out, block):
    frames, contacts = own.shape
    width = 2 * v4[0].shape[-1]
    tile = 256
    visitors = [*vx, *v2, *vy, *v4]
    aliased = out is not None
    in_specs = [
        pl.BlockSpec(memory_space=pltpu.SMEM),
        pl.BlockSpec((tile, contacts), lambda i: (i, 0)),
        pl.BlockSpec((tile, 1), lambda i: (i, 0)),
    ] + block_specs(visitors)
    args = [bit, own, norms, *visitors]
    if aliased:
        in_specs.append(pl.BlockSpec(memory_space=pl.ANY))
        args.append(out)
    return pl.pallas_call(
        functools.partial(distance_kernel, aliased=aliased),
        grid=(frames // tile,),
        in_specs=in_specs,
        out_specs=[
            pl.BlockSpec((ROUNDS, tile, width), lambda i: (0, i, block)),
            pl.BlockSpec((8, 128), lambda i: (0, 0)),
        ],
        out_shape=[
            jax.ShapeDtypeStruct((ROUNDS, frames, frames), jnp.bfloat16),
            jax.ShapeDtypeStruct((8, 128), jnp.float32),
        ],
        scratch_shapes=[pltpu.VMEM((ROUNDS, 8, width), jnp.float32)],
        input_output_aliases={len(args) - 1: 0} if aliased else {},
        compiler_params=pltpu.CompilerParams(vmem_limit_bytes=VMEM_BYTES),
    )(*args)


def half_kernel(places_ref, own_ref, norm_ref, *refs):
    visitors = [refs[:2], refs[2:4]]
    out_ref, token_ref, vnorm_ref = refs[5:]
    token_ref[...] = jnp.zeros_like(token_ref)
    for which, pair in enumerate(visitors):
        @pl.when(pl.program_id(0) == which)
        def _(pair=pair):
            @pl.when(pl.program_id(1) == 0)
            def _():
                vnorm_ref[0:1, :] = column_norms(side_by_side(pair))

            out_ref[0] = tanimoto(own_ref, norm_ref, side_by_side(pair), vnorm_ref[0:1, :])


def distance_half(places, own, norms, first, second, out, block):
    frames, contacts = own.shape
    width = 2 * first[0].shape[-1]
    tile = 512
    visitors = [*first, *second]
    in_specs = [
        pl.BlockSpec((tile, contacts), lambda r, i, p: (i, 0)),
        pl.BlockSpec((tile, 1), lambda r, i, p: (i, 0)),
    ] + block_specs(visitors) + [pl.BlockSpec(memory_space=pl.ANY)]
    return pl.pallas_call(
        half_kernel,
        grid_spec=pltpu.PrefetchScalarGridSpec(
            num_scalar_prefetch=1,
            grid=(2, frames // tile),
            in_specs=in_specs,
            out_specs=[
                pl.BlockSpec((1, tile, width), lambda r, i, p: (p[r], i, block)),
                pl.BlockSpec((8, 128), lambda r, i, p: (0, 0)),
            ],
            scratch_shapes=[pltpu.VMEM((8, width), jnp.float32)],
        ),
        out_shape=[
            jax.ShapeDtypeStruct((ROUNDS, frames, frames), jnp.bfloat16),
            jax.ShapeDtypeStruct((8, 128), jnp.float32),
        ],
        input_output_aliases={7: 0},
        compiler_params=pltpu.CompilerParams(vmem_limit_bytes=VMEM_BYTES),
        name="distances_half",
    )(places, own, norms, *visitors, out)


def contact_slots(pairs, res_slot):
    hits = pairs[:, :, None] == res_slot[None, None, :]
    places = jnp.arange(res_slot.shape[0], dtype=jnp.int32)
    return jnp.sum(jnp.where(hits, places, 0), axis=2, dtype=jnp.int32)


def split_kernel(x_ref, pieces_ref, extent_ref, spread_ref):
    step = pl.program_id(0)
    _, _, _, frames = pieces_ref.shape
    per_step = x_ref.shape[2] // frames

    @pl.when(step == 0)
    def _():
        extent_ref[...] = jnp.zeros_like(extent_ref)
        spread_ref[...] = jnp.full_like(spread_ref, jnp.inf)

    for k in range(per_step):
        x = x_ref[:, :, k * frames:(k + 1) * frames]
        coded = jnp.clip(jnp.round(x * (1.0 / UNIT)), -32767.0, 32767.0)
        pieces_ref[step * per_step + k] = coded.astype(jnp.int32).astype(jnp.int16)
        extent_ref[...] = jnp.maximum(extent_ref[...], jnp.max(jnp.abs(x), axis=0))
        mean = jnp.sum(x, axis=2, keepdims=True) * (1.0 / frames)
        square = jnp.sum(x * x, axis=2, keepdims=True) * (1.0 / frames)
        spread = jnp.mean(square - mean * mean, axis=(0, 1), keepdims=True)[0]
        spread_ref[...] = jnp.minimum(spread_ref[...], spread)

    @pl.when(step == pl.num_programs(0) - 1)
    def _():
        fine = (jnp.max(extent_ref[...]) <= 32767.0 * UNIT) & (jnp.min(spread_ref[...]) >= 0.05)

        @pl.when(jnp.logical_not(fine))
        def _():
            pieces_ref[...] = jnp.full(pieces_ref.shape, BAD, jnp.int32).astype(jnp.int16)


def split_blocks(coords, count):
    _, rows, frames = coords.shape
    per_block = frames // count
    per_step = largest_divisor(count, 4)
    return pl.pallas_call(
        split_kernel,
        grid=(count // per_step,),
        in_specs=[pl.BlockSpec((3, rows, per_step * per_block), lambda i: (0, 0, i))],
        out_specs=pl.BlockSpec((count, 3, rows, per_block), lambda i: (0, 0, 0, 0)),
        out_shape=jax.ShapeDtypeStruct((count, 3, rows, per_block), jnp.int16),
        scratch_shapes=[pltpu.VMEM((rows, per_block), jnp.float32), pltpu.VMEM((1, 1), jnp.float32)],
        compiler_params=pltpu.CompilerParams(vmem_limit_bytes=58 * 1024 * 1024),
        name="split_blocks",
    )(coords)


def exchanged(pieces):
    got = lax.all_to_all(pieces, "blocks", split_axis=0, concat_axis=0, tiled=True)
    count, _, rows, per_block = got.shape
    if rows % 8:
        got = got.transpose(0, 2, 1, 3).reshape(count * rows // 8, 8, 3, per_block)
        got = got.transpose(0, 2, 1, 3)
    return got


def contact_features(coords, slots24, starts, widths):
    count = lax.axis_size("blocks")
    narrow = exchanged(split_blocks(coords.transpose(1, 0, 2), count))
    all_fine = jnp.all(narrow[:, 0, 0, 0] != BAD)

    def coarse():
        return features_of(narrow, slots24, starts, widths, UNIT)

    def exact():
        pieces = coords.reshape(coords.shape[0], 3, count, -1).transpose(2, 1, 0, 3)
        return features_of(exchanged(pieces), slots24, starts, widths, 1.0)

    return lax.cond(all_fine, coarse, exact)


def shards(coords, pairs, res_slot):
    index = lax.axis_index("blocks")
    lanes = coords.shape[2] // lax.axis_size("blocks") // CHUNKS
    widths = [lanes] * CHUNKS
    starts = [lanes * n for n in range(CHUNKS)]

    slots24 = contact_slots(pairs, res_slot).reshape(-1) * 24
    fts = contact_features(coords, slots24, starts, widths)

    bit = (index & 1).astype(jnp.int32).reshape(1)
    low_core = 1 - bit
    low_pair = 1 - ((index >> 1) & 1).astype(jnp.int32).reshape(1)

    v4s = []
    for ft in fts:
        v4s.append(permuted(ft, "blocks", shift4))
    own, norms = own_features(fts, starts)

    out = None
    tokens = []
    for p in range(CHUNKS // 2):
        both = (2 * p, 2 * p + 1)
        after = tokens[p - 2:p - 1] if p >= 2 else [norms]
        v2 = []
        for k in both:
            sent = pick(low_pair, [fts[k]], [v4s[k]], after)
            v2.append(permuted(sent, "blocks", swap2))
        sent = pick(low_core, [fts[k] for k in both], [v4s[k] for k in both], [])
        vy = permuted(sent, "blocks", swap1)
        vy = [vy[0], vy[1]]
        vx = []
        for k in both:
            vx.append(permuted(v2[k - 2 * p], "blocks", swap1))
        v4 = [v4s[k] for k in both]
        if p + 1 < CHUNKS // 2:
            out, token = distance_pair(bit, own, norms, vx, v2, vy, v4, out, p)
            tokens.append(token)
        else:
            places = jnp.concatenate([jnp.full((1,), 3, jnp.int32), 2 - 2 * bit])
            out, _ = distance_half(places, own, norms, v4, vy, out, p)
            places = jnp.concatenate([jnp.full((1,), 1, jnp.int32), 2 * bit])
            out, _ = distance_half(places, own, norms, v2, vx, out, p)
    return out


def solution(mesh):
    in_specs = (P("blocks", None, "parts"), P(), P())
    out_specs = P(None, ("parts", "blocks"), None)
    return jax.shard_map(shards, mesh=mesh, in_specs=in_specs, out_specs=out_specs, check_vma=False)
```
